32 devices in a mesh: groups: 2 (over y), pts: 4 (over z), freq: 2 (over x), sub: 2 (over core).
Axes of the slice: x: 2, y: 2, z: 4, core: 2. Of those that a mesh axis runs over, the one named last changes fastest.
Arguments:
- series: bfloat16 [2048, 8, 16384], P(('pts', 'sub'), 'freq', 'groups'), parts along dimension 2, may hold values from -256 to 256, as said below
- block_start: int32 [15], replicated, may hold values from 0 to 1792, as said below
- freq_index: int32 [64], replicated, may hold values from 0 to 128, as said below
Outputs:
- modes: float32 [2, 64, 16, 8192], P(None, 'freq', 'groups', ('pts', 'sub')), parts along dimension 2
- spectrum: float32 [128], P(('groups', 'freq')), parts along dimension 0
The draws below stay inside these ranges and needn't reach their ends.
There are 2 independent parts, one for each index of `groups`. The reference program is written for one: setup_inputs(seed, part) draws one part's arguments, and reference() takes and returns one part's arrays. A program takes and returns all parts, laid end to end along the dimension named above; an argument that names none is the same for every part. Nothing has to cross between parts.
Inputs may be any that keep to these rules, and one draw needn't show every extreme that they name: series is finite. block_start rises with the block; its first entry is 0 and its last is 1792; every other entry lies within 32 of its block number times 128. freq_index holds 64 different bins, 0 and 128 among them.
All inputs are finite; a program needn't handle non-finite values.
Results may differ from the reference program's by a relative error of at most 0.0041.
Values may be sent and summed in bfloat16 or wider, within the bound.
No kernel may reach another device: no remote copies, remote signals or barrier semaphores. Data moves between devices by JAX's collectives and lax.ppermute only.
A program may use at most 128 MiB of HBM per device.

```python
import math
import jax
import jax.numpy as jnp
from jax import lax

NFFT = 256
BLOCKS = 15
NF = 64
GX = 8
GR = 8192
ITERS = 3
SEGMENT_SPACING = 128
FRAME_TOTAL = 2048


def exponent_flat_draw(key, shape, lower, upper):
    return jnp.exp(jax.random.uniform(key, shape, jnp.float32, math.log(lower), math.log(upper)))


def draw_series(key, part):
    key = jax.random.fold_in(key, 101)
    disturbance_seed_handle, location_seed_handle, pulse_seed_handle, oscillation_seed_handle = jax.random.split(key, 4)
    wave_keys = jax.random.split(oscillation_seed_handle, 7)
    wave_count = 6
    noise_draw = jax.random.normal(disturbance_seed_handle, (FRAME_TOTAL, GX, GR), jnp.float32)
    point_scale = exponent_flat_draw(location_seed_handle, (GX, GR), 0.3, 3.0)
    magnitude_profile = exponent_flat_draw(pulse_seed_handle, (FRAME_TOTAL // SEGMENT_SPACING,), 0.5, 2.0)
    rising = 3.0
    strength = exponent_flat_draw(wave_keys[2], (wave_count,), 0.25, 0.7)
    segment_amp = exponent_flat_draw(wave_keys[3], (wave_count, FRAME_TOTAL // SEGMENT_SPACING), 0.4, 2.5)
    position = jnp.arange(GR, dtype=jnp.float32) / (GR - 1)
    point_scale = point_scale * jnp.power(rising, position)[None, :]
    magnitude_profile = jnp.repeat(magnitude_profile, SEGMENT_SPACING)
    total = noise_draw * magnitude_profile[:, None, None] * point_scale[None, :, :]
    wave_freq = jax.random.uniform(wave_keys[0], (wave_count,), jnp.float32, 2.0, NFFT / 2.0 - 2.0) / NFFT
    center = jax.random.uniform(wave_keys[1], (wave_count,), jnp.float32, 0.1, 0.9)
    wave_x = jax.random.randint(wave_keys[4], (wave_count,), 1, 4, jnp.int32).astype(jnp.float32)
    wave_r = jax.random.randint(wave_keys[5], (wave_count,), 2, 9, jnp.int32).astype(jnp.float32)
    jitter = jax.random.uniform(wave_keys[6], (wave_count, GX, GR), jnp.float32, -0.6, 0.6)
    snap_time = jnp.arange(FRAME_TOTAL, dtype=jnp.float32)
    x_place = jnp.arange(GX, dtype=jnp.float32) / GX
    for wave in range(wave_count):
        offset = (position - center[wave]) / 0.08
        bump = jnp.exp(-0.5 * offset * offset)
        amp_time = jnp.repeat(segment_amp[wave], SEGMENT_SPACING) * strength[wave]
        space_phase = 2.0 * math.pi * (wave_x[wave] * x_place[:, None] + wave_r[wave] * position[None, :]) + jitter[wave]
        cycles = jnp.mod(wave_freq[wave] * snap_time, 1.0)
        shape_space = bump[None, :] * point_scale
        total = total + amp_time[:, None, None] * shape_space[None, :, :] * jnp.cos(2.0 * math.pi * cycles[:, None, None] - space_phase[None, :, :])
    return total.astype(jnp.bfloat16)


def draw_block_start(key, part):
    key = jax.random.fold_in(key, 202)
    jitter = jax.random.randint(key, (BLOCKS,), -(SEGMENT_SPACING // 4), SEGMENT_SPACING // 4 + 1, jnp.int32)
    number = jnp.arange(BLOCKS, dtype=jnp.int32)
    inside = (number > 0) & (number < BLOCKS - 1)
    return number * SEGMENT_SPACING + jnp.where(inside, jitter, 0)


def draw_freq_index(key, part):
    key = jax.random.fold_in(key, 303)
    pick_key, order_key = jax.random.split(key)
    middle = jax.random.permutation(pick_key, NFFT // 2 - 1)[:NF - 2].astype(jnp.int32) + 1
    chosen = jnp.concatenate([jnp.array([0, NFFT // 2], dtype=jnp.int32), middle])
    return chosen[jax.random.permutation(order_key, NF)]


def setup_inputs(seed: int = 0, part: int = 0) -> dict:
    key_of = jax.random.split(jax.random.key(seed), 4)
    part_keys = jax.random.split(jax.random.fold_in(key_of[3], part), 4)
    return {
        "series": draw_series(jax.random.fold_in(jax.random.fold_in(key_of[3], part), 71), part),
        "block_start": draw_block_start(jax.random.fold_in(key_of[3], 71), part),
        "freq_index": draw_freq_index(jax.random.fold_in(key_of[3], 71), part),
    }


def dft_basis(freq_index, window_len):
    steps_int = jnp.arange(window_len, dtype=jnp.int32)
    phase_int = freq_index[:, None] * steps_int[None, :] % window_len
    angle = 2.0 * math.pi / window_len * phase_int.astype(jnp.float32)
    window = 0.5 - 0.5 * jnp.cos(2.0 * math.pi / window_len * steps_int.astype(jnp.float32))
    weighting = window / jnp.sqrt(jnp.sum(window * window))
    table = jnp.stack([jnp.cos(angle), -jnp.sin(angle)], axis=1) * weighting[None, None, :]
    return table.reshape(-1, window_len).astype(jnp.bfloat16)

def apply_cross(cross_real, cross_imag, vec_real, vec_imag):
    highest = lax.Precision.HIGHEST
    out_real = jnp.einsum('kbd,kd->kb', cross_real, vec_real, precision=highest) - jnp.einsum('kbd,kd->kb', cross_imag, vec_imag, precision=highest)
    out_imag = jnp.einsum('kbd,kd->kb', cross_real, vec_imag, precision=highest) + jnp.einsum('kbd,kd->kb', cross_imag, vec_real, precision=highest)
    return (out_real, out_imag)

def leading_vector(cross_real, cross_imag, sweeps):
    initial = jnp.full(cross_real.shape[:2], 1.0 / math.sqrt(cross_real.shape[1]), jnp.float32)
    vec_real = initial
    vec_imag = jnp.zeros_like(initial)
    for sweep_index in range(sweeps):
        out_real, out_imag = apply_cross(cross_real, cross_imag, vec_real, vec_imag)
        length = jnp.sqrt(lax.optimization_barrier(jnp.sum(out_real * out_real + out_imag * out_imag, axis=1, keepdims=True)))
        vec_real = out_real / length
        vec_imag = out_imag / length
    out_real, out_imag = apply_cross(cross_real, cross_imag, vec_real, vec_imag)
    spectrum = lax.optimization_barrier(jnp.sum(vec_real * out_real + vec_imag * out_imag, axis=1))
    return (vec_real, vec_imag, spectrum)

def reference(series, block_start, freq_index):
    snap_rows, slab_rows, plane = series.shape
    blocks = block_start.shape[0]
    retained = freq_index.shape[0]
    total_points = slab_rows * plane
    history = series.reshape(snap_rows, total_points)
    basis = dft_basis(freq_index, NFFT)

    def one_block(carried, offset):
        segment = lax.dynamic_slice_in_dim(history, offset, NFFT, 0)
        return (carried, jnp.dot(basis, segment, preferred_element_type=jnp.float32).astype(jnp.bfloat16))
    unused, tiles = lax.scan(one_block, jnp.int32(0), block_start)
    coefficients = tiles.reshape(blocks, retained, 2, slab_rows, plane)
    highest = lax.Precision.HIGHEST

    def gram_one(index):
        tile = lax.dynamic_index_in_dim(coefficients, index, 1, keepdims=False).astype(jnp.float32)
        product = jnp.einsum('bcxr,dexr->cebd', tile, tile, precision=highest)
        return (product[0, 0] + product[1, 1], product[0, 1] - product[1, 0])
    frequency_ids = jnp.arange(retained, dtype=jnp.int32)
    cross_real, cross_imag = lax.map(gram_one, frequency_ids)
    norm_scale = 1.0 / (blocks * total_points)
    cross_real = cross_real * norm_scale
    cross_imag = cross_imag * norm_scale
    vec_real, vec_imag, spectrum = leading_vector(cross_real, cross_imag, ITERS)
    low_real = vec_real.astype(jnp.bfloat16)
    low_imag = vec_imag.astype(jnp.bfloat16)

    def mode_one(index):
        tile = lax.dynamic_index_in_dim(coefficients, index, 1, keepdims=False).astype(jnp.float32)
        part_real = lax.dynamic_index_in_dim(low_real, index, 0, keepdims=False)
        part_imag = lax.dynamic_index_in_dim(low_imag, index, 0, keepdims=False)
        mixing = jnp.stack([jnp.stack([part_real, part_imag], axis=0), jnp.stack([-part_imag, part_real], axis=0)], axis=0).astype(jnp.float32)
        return jnp.einsum('bcxr,ceb->exr', tile, mixing, precision=highest)
    raw_stack = lax.map(mode_one, frequency_ids)
    raw_modes = jnp.transpose(raw_stack, (1, 0, 2, 3))
    energy = lax.optimization_barrier(jnp.sum(raw_modes[0] * raw_modes[0] + raw_modes[1] * raw_modes[1], axis=(1, 2))) / total_points
    modes = raw_modes * lax.rsqrt(energy + 1e-06)[None, :, None, None]
    return (modes, spectrum)
```

```python
import functools
import math

import jax
import jax.numpy as jnp
from jax import lax
from jax.experimental import pallas as pl
from jax.experimental.pallas import tpu as pltpu
from jax.sharding import PartitionSpec as P

NFFT = 256
ITERS = 3
SPAN = 2 * NFFT
LANES = 128
SUBLANES = 8
GROUP_ROWS = 2 * SUBLANES
MIB = 1 << 20


def shifted_basis(freq_order, offsets, blocks):
    steps = jnp.arange(SPAN, dtype=jnp.int32)[None, :] - offsets[:, None]
    inside = (steps >= 0) & (steps < NFFT) & (jnp.arange(offsets.shape[0]) < blocks)[:, None]
    steps = jnp.where(inside, steps, 0)
    unit = 2.0 * math.pi / NFFT
    window = 0.5 - 0.5 * jnp.cos(unit * jnp.arange(NFFT, dtype=jnp.int32).astype(jnp.float32))
    shifted_window = 0.5 - 0.5 * jnp.cos(unit * steps.astype(jnp.float32))
    weighting = jnp.where(inside, shifted_window / jnp.sqrt(jnp.sum(window * window)), 0.0)
    freq = freq_order.reshape(1, -1, SUBLANES, 1)
    phase_int = freq * steps[:, None, None, :] % NFFT
    angle = unit * phase_int.astype(jnp.float32)
    table = jnp.stack([jnp.cos(angle), -jnp.sin(angle)], axis=2) * weighting[:, None, None, None, :]
    return table.astype(jnp.bfloat16).reshape(offsets.shape[0] // 2, -1, SPAN)


def spectra_kernel(window_start, history, basis, total_in, *outs, members):
    coefs = outs[:members]
    total_out = outs[members]
    rows = coefs[0].shape[1]
    pairs = basis.shape[0]
    width = history.shape[1]
    for pair in range(pairs):
        start = pl.multiple_of(window_start[pair], 16)
        segment = history[pl.ds(start, SPAN), :]
        both = jnp.dot(basis[pair], segment, preferred_element_type=jnp.float32)
        both = both.astype(jnp.bfloat16)
        for half in range(2):
            for member in range(members):
                first = (half * members + member) * rows
                coefs[member][2 * pair + half] = both[first : first + rows]
    lane = lax.broadcasted_iota(jnp.int32, (2 * pairs * SUBLANES, LANES), 1)
    sub = lax.broadcasted_iota(jnp.int32, (2 * pairs * SUBLANES, LANES), 0) % SUBLANES
    place = (lane - sub) & (LANES - 1)
    for member in range(members):
        packed = [jnp.zeros((2 * pairs * SUBLANES, LANES), jnp.float32) for _ in range(2)]
        for group in range(rows // GROUP_ROWS):
            tile = coefs[member][:, group * GROUP_ROWS : (group + 1) * GROUP_ROWS, :]
            tile = tile.reshape(2 * pairs * GROUP_ROWS, width)
            gram = lax.dot_general(
                tile, tile, (((1,), (1,)), ((), ())), preferred_element_type=jnp.float32
            )
            gram = gram.reshape(2 * pairs, 2, SUBLANES, 2 * LANES)
            for c in range(2):
                for high in range(2):
                    shift = group + 4 * high
                    part = gram[:, c, :, high * LANES : (high + 1) * LANES]
                    part = part.reshape(2 * pairs * SUBLANES, LANES)
                    part = pltpu.roll(part, shift, 1) if shift else part
                    packed[c] = jnp.where(place % 8 == shift, part, packed[c])
        swapped = jnp.where(
            (place // 8) % 2 == 0,
            pltpu.roll(packed[1], LANES - 8, 1),
            -pltpu.roll(packed[1], 8, 1),
        )
        total_out[member] = total_in[member] + (packed[0] + swapped)


def spectra(window_start, history, basis, total, members):
    width = history.shape[1]
    blocks = 2 * basis.shape[0]
    rows = basis.shape[1] // 2 // members
    vmem = pl.BlockSpec(memory_space=pltpu.VMEM)
    outs = [jax.ShapeDtypeStruct((blocks, rows, width), jnp.bfloat16)] * members
    return pl.pallas_call(
        functools.partial(spectra_kernel, members=members),
        out_shape=outs + [jax.ShapeDtypeStruct(total.shape, jnp.float32)],
        in_specs=[pl.BlockSpec(memory_space=pltpu.SMEM), vmem, vmem, vmem],
        out_specs=[vmem] * (members + 1),
        compiler_params=pltpu.CompilerParams(vmem_limit_bytes=40 * MIB),
        cost_estimate=pl.CostEstimate(
            flops=2 * blocks * members * rows * width * (SPAN + 256),
            bytes_accessed=2 * (history.size + basis.size + blocks * members * rows * width),
            transcendentals=0,
        ),
        name="spectra",
    )(window_start, history, basis, total)


def power_kernel(total, mix, scale, spectrum, *, blocks, norm_scale):
    padded = total.shape[0] // SUBLANES
    cross = total[...].reshape(padded, SUBLANES, LANES) * norm_scale
    shape = (SUBLANES, LANES)
    lane = lax.broadcasted_iota(jnp.int32, shape, 1)
    sub = lax.broadcasted_iota(jnp.int32, shape, 0)
    place = (lane - sub) & (LANES - 1)
    number = place // 16 + 8 * ((place // 4) % 2)
    is_real = (place // 8) % 2 == 0

    def lane_sum(value):
        for shift in (64, 32, 16, 8, 4):
            value = value + pltpu.roll(value, shift, value.ndim - 1)
        return value

    def turned(vec):
        for_real = jnp.where(is_real, vec, -vec)
        for_imag = jnp.where(is_real, pltpu.roll(vec, LANES - 8, 1), pltpu.roll(vec, 8, 1))
        return for_real, for_imag

    def apply(vec):
        for_real, for_imag = turned(vec)
        out_real = lane_sum(cross * for_real[None])
        out_imag = lane_sum(cross * for_imag[None])
        out = jnp.zeros(shape, jnp.float32)
        for block in range(padded):
            out = jnp.where(number == block, jnp.where(is_real, out_real[block], out_imag[block]), out)
        return out

    vec = jnp.where(is_real & (number < blocks), 1.0 / math.sqrt(blocks), 0.0)
    for _ in range(ITERS):
        out = apply(vec)
        vec = out / jnp.sqrt(lane_sum(out * out))
    value = lane_sum(vec * apply(vec))
    low = vec.astype(jnp.bfloat16).astype(jnp.float32)
    energy = lane_sum(low * apply(low)) * blocks
    factor = lax.rsqrt(jnp.maximum(energy, 0.0) + 1e-06)

    def spread(values, group):
        picked = jnp.where(place % 4 == group, values, 0.0)
        picked = picked + pltpu.roll(picked, 1, 1)
        return picked + pltpu.roll(picked, 2, 1)

    for_real, for_imag = turned(low)
    diagonal = lane % SUBLANES == sub
    for group in range(mix.shape[0]):
        parts = []
        for vec_part in (for_real, for_imag):
            row = []
            for high in range(2):
                shift = (LANES - group - 4 * high) % LANES
                moved = pltpu.roll(vec_part, shift, 1) if shift else vec_part
                row.append(jnp.where(diagonal, moved, 0.0))
            parts.append(jnp.concatenate(row, axis=1))
        mix[group] = jnp.concatenate(parts, axis=0).astype(jnp.bfloat16)
        scale[group] = spread(factor, group)
        spectrum[group] = spread(value, group)


def leading_vectors(total, groups, blocks, norm_scale):
    vmem = pl.BlockSpec(memory_space=pltpu.VMEM)
    return pl.pallas_call(
        functools.partial(power_kernel, blocks=blocks, norm_scale=norm_scale),
        out_shape=[
            jax.ShapeDtypeStruct((groups, GROUP_ROWS, 2 * LANES), jnp.bfloat16),
            jax.ShapeDtypeStruct((groups, SUBLANES, LANES), jnp.float32),
            jax.ShapeDtypeStruct((groups, SUBLANES, LANES), jnp.float32),
        ],
        in_specs=[vmem],
        out_specs=[vmem] * 3,
        name="power",
    )(total)


def modes_kernel(member_ref, mix, scale, *refs, chunks, members):
    coefs = refs[: chunks * members]
    out, buffer, sems = refs[chunks * members :]
    member = member_ref[0]
    copies = []
    for chunk in range(chunks):
        for turn in range(members):
            slot = lax.rem(member + members - turn, members)
            copy = pltpu.make_async_copy(
                coefs[chunk * members + turn], buffer.at[chunk, slot], sems.at[chunk, turn]
            )
            copy.start()
            copies.append(copy)
    width = coefs[0].shape[2]
    padded = coefs[0].shape[0]
    planes = out.shape[2] // members
    points = width // planes
    for chunk in range(chunks):
        for turn in range(members):
            copies[chunk * members + turn].wait()
        for slot in range(members):
            for group in range(mix.shape[0]):
                tile = buffer[chunk, slot, :, group * GROUP_ROWS : (group + 1) * GROUP_ROWS, :]
                tile = tile.reshape(padded * GROUP_ROWS, width)
                raw = jnp.dot(mix[group], tile, preferred_element_type=jnp.float32)
                for e in range(2):
                    for plane in range(planes):
                        part = raw[
                            e * SUBLANES : (e + 1) * SUBLANES, plane * points : (plane + 1) * points
                        ]
                        out[
                            e,
                            group * SUBLANES : (group + 1) * SUBLANES,
                            slot * planes + plane,
                            chunk * points : (chunk + 1) * points,
                        ] = part * jnp.tile(scale[group], (1, points // LANES))


def project(member, mix, scale, coefs, members, planes, points):
    chunks = len(coefs) // members
    groups = mix.shape[0]
    vmem = pl.BlockSpec(memory_space=pltpu.VMEM)
    return pl.pallas_call(
        functools.partial(modes_kernel, chunks=chunks, members=members),
        out_shape=jax.ShapeDtypeStruct(
            (2, groups * SUBLANES, members * planes, points), jnp.float32
        ),
        in_specs=[pl.BlockSpec(memory_space=pltpu.SMEM), vmem, vmem]
        + [pl.BlockSpec(memory_space=pl.ANY)] * len(coefs),
        out_specs=vmem,
        scratch_shapes=[
            pltpu.VMEM((chunks, members) + coefs[0].shape, jnp.bfloat16),
            pltpu.SemaphoreType.DMA((chunks, members)),
        ],
        compiler_params=pltpu.CompilerParams(vmem_limit_bytes=48 * MIB),
        name="modes",
    )(member, mix, scale, *coefs)


def butterfly_sum(value, axes, count):
    step = 1
    while step < count:
        pairs = [(i, i ^ step) for i in range(count)]
        value = value + lax.ppermute(value, axes, pairs)
        step *= 2
    return value


def shards(series, block_start, freq_index):
    snap_rows, slab_rows, plane = series.shape
    line = ("pts", "sub")
    group_count = lax.axis_size(line)
    members = lax.axis_size("freq")
    member = lax.axis_index("freq")
    width = plane // group_count
    chunk_points = LANES
    chunks = width // chunk_points
    blocks = block_start.shape[0]
    pairs = (blocks + 1) // 2
    frames = snap_rows * group_count

    order = (member + jnp.arange(members, dtype=jnp.int32)) % members
    freq_order = freq_index.reshape(members, -1)[order].reshape(-1)
    starts = jnp.pad(block_start, (0, 2 * pairs - blocks), mode="edge")
    window_start = jnp.minimum(starts[::2] // 16 * 16, frames - SPAN)
    basis = shifted_basis(freq_order, starts - jnp.repeat(window_start, 2), blocks)

    tiles = series.reshape(snap_rows, slab_rows, group_count, chunks, chunk_points)
    total = jnp.zeros((members, 2 * pairs * SUBLANES, LANES), jnp.float32)
    coefs = []
    for chunk in range(chunks):
        piece = jnp.transpose(tiles[:, :, :, chunk, :], (2, 0, 1, 3))
        piece = piece.reshape(group_count, snap_rows, slab_rows * chunk_points)
        history = lax.all_to_all(piece, line, split_axis=0, concat_axis=0, tiled=True)
        history = history.reshape(frames, slab_rows * chunk_points)
        *sent, total = spectra(window_start, history, basis, total, members)
        coefs.append(sent[0])
        for turn in range(1, members):
            ring = [(i, (i + turn) % members) for i in range(members)]
            coefs.append(lax.ppermute(sent[turn], "freq", ring))

    mine = total[0]
    for turn in range(1, members):
        ring = [(i, (i + turn) % members) for i in range(members)]
        mine = mine + lax.ppermute(total[turn], "freq", ring)
    mine = butterfly_sum(mine, line, group_count)

    groups = freq_index.shape[0] // members // SUBLANES
    norm_scale = 1.0 / (blocks * slab_rows * members * plane)
    mix, scale, spectrum = leading_vectors(mine, groups, blocks, norm_scale)
    modes = project(member.reshape(1), mix, scale, coefs, members, slab_rows, width)
    return (modes, spectrum[:, :, 0].reshape(-1))


def solution(mesh):
    in_specs = (P(("pts", "sub"), "freq", "groups"), P(), P())
    out_specs = (P(None, "freq", "groups", ("pts", "sub")), P(("groups", "freq")))
    return jax.shard_map(shards, mesh=mesh, in_specs=in_specs, out_specs=out_specs, check_vma=False)
```

```python
import functools
import math

import jax
import jax.numpy as jnp
from jax import lax
from jax.experimental import pallas as pl
from jax.experimental.pallas import tpu as pltpu
from jax.sharding import PartitionSpec as P

NFFT = 256
ITERS = 3
SPAN = 2 * NFFT
LANES = 128
SUBLANES = 8
AHEAD = 2
GROUP_ROWS = 2 * SUBLANES
MIB = 1 << 20


def shifted_basis(freq_order, offsets, blocks):
    steps = jnp.arange(SPAN, dtype=jnp.int32)[None, :] - offsets[:, None]
    inside = (steps >= 0) & (steps < NFFT) & (jnp.arange(offsets.shape[0]) < blocks)[:, None]
    steps = jnp.where(inside, steps, 0)
    unit = 2.0 * math.pi / NFFT
    window = 0.5 - 0.5 * jnp.cos(unit * jnp.arange(NFFT, dtype=jnp.int32).astype(jnp.float32))
    shifted_window = 0.5 - 0.5 * jnp.cos(unit * steps.astype(jnp.float32))
    weighting = jnp.where(inside, shifted_window / jnp.sqrt(jnp.sum(window * window)), 0.0)
    freq = freq_order.reshape(1, -1, SUBLANES, 1)
    phase_int = freq * steps[:, None, None, :] % NFFT
    angle = unit * phase_int.astype(jnp.float32)
    table = jnp.stack([jnp.cos(angle), -jnp.sin(angle)], axis=2) * weighting[:, None, None, None, :]
    return table.astype(jnp.bfloat16).reshape(offsets.shape[0] // 2, -1, SPAN)


def prepare_kernel(line_ref, *refs, count):
    del line_ref
    for piece in range(count):
        source, target = refs[piece], refs[count + piece]
        points = source.shape[2]
        for plane in range(source.shape[1]):
            target[:, plane * points : (plane + 1) * points] = source[:, plane, :]


def prepare(line_index, series, offset, points, count):
    snap_rows, slab_rows, plane = series.shape
    first, stride = offset // points, plane // count // points

    def source_map(piece):
        return lambda step, line_ref: (0, 0, (line_ref[0] ^ piece) * stride + first)

    return pl.pallas_call(
        functools.partial(prepare_kernel, count=count),
        grid_spec=pltpu.PrefetchScalarGridSpec(
            num_scalar_prefetch=1,
            grid=(1,),
            in_specs=[
                pl.BlockSpec((snap_rows, slab_rows, points), source_map(piece))
                for piece in range(count)
            ],
            out_specs=[
                pl.BlockSpec((snap_rows, slab_rows * points), lambda step, line_ref: (0, 0))
                for piece in range(count)
            ],
        ),
        out_shape=[jax.ShapeDtypeStruct((snap_rows, slab_rows * points), series.dtype)] * count,
        compiler_params=pltpu.CompilerParams(vmem_limit_bytes=40 * MIB),
        cost_estimate=pl.CostEstimate(
            flops=0, bytes_accessed=4 * count * snap_rows * slab_rows * points, transcendentals=0
        ),
        name="prepare",
    )(line_index, *([series] * count))


def spectra_kernel(line_ref, window_start, basis, total_in, *refs, count, members):
    pieces = refs[:count]
    coefs = refs[count : count + members]
    total_out, history, sems = refs[count + members :]
    copies = []
    for piece in range(count):
        length = pieces[piece].shape[0]
        first = pl.multiple_of((line_ref[0] ^ piece) * length if count > 1 else 0, 16)
        copies.append(
            pltpu.make_async_copy(pieces[piece], history.at[pl.ds(first, length)], sems.at[piece])
        )
        copies[-1].start()
    for copy in copies:
        copy.wait()
    rows = coefs[0].shape[1]
    pairs = basis.shape[0]
    width = history.shape[1]
    for pair in range(pairs):
        start = pl.multiple_of(window_start[pair], 16)
        segment = history[pl.ds(start, SPAN), :]
        both = jnp.dot(basis[pair], segment, preferred_element_type=jnp.float32)
        both = both.astype(jnp.bfloat16)
        for half in range(2):
            for member in range(members):
                first = (half * members + member) * rows
                coefs[member][2 * pair + half] = both[first : first + rows]
    lane = lax.broadcasted_iota(jnp.int32, (2 * pairs * SUBLANES, LANES), 1)
    sub = lax.broadcasted_iota(jnp.int32, (2 * pairs * SUBLANES, LANES), 0) % SUBLANES
    place = (lane - sub) & (LANES - 1)
    for member in range(members):
        packed = [jnp.zeros((2 * pairs * SUBLANES, LANES), jnp.float32) for _ in range(2)]
        for group in range(rows // GROUP_ROWS):
            tile = coefs[member][:, group * GROUP_ROWS : (group + 1) * GROUP_ROWS, :]
            tile = tile.reshape(2 * pairs * GROUP_ROWS, width)
            gram = lax.dot_general(
                tile, tile, (((1,), (1,)), ((), ())), preferred_element_type=jnp.float32
            )
            gram = gram.reshape(2 * pairs, 2, SUBLANES, 2 * LANES)
            for c in range(2):
                for high in range(2):
                    shift = group + 4 * high
                    part = gram[:, c, :, high * LANES : (high + 1) * LANES]
                    part = part.reshape(2 * pairs * SUBLANES, LANES)
                    part = pltpu.roll(part, shift, 1) if shift else part
                    packed[c] = jnp.where(place % 8 == shift, part, packed[c])
        swapped = jnp.where(
            (place // 8) % 2 == 0,
            pltpu.roll(packed[1], LANES - 8, 1),
            -pltpu.roll(packed[1], 8, 1),
        )
        total_out[member] = total_in[member] + (packed[0] + swapped)


def spectra(line_index, window_start, pieces, basis, total, members):
    count = len(pieces)
    length, width = pieces[0].shape
    blocks = 2 * basis.shape[0]
    rows = basis.shape[1] // 2 // members
    smem = pl.BlockSpec(memory_space=pltpu.SMEM)
    vmem = pl.BlockSpec(memory_space=pltpu.VMEM)
    outs = [jax.ShapeDtypeStruct((blocks, rows, width), jnp.bfloat16)] * members
    return pl.pallas_call(
        functools.partial(spectra_kernel, count=count, members=members),
        out_shape=outs + [jax.ShapeDtypeStruct(total.shape, jnp.float32)],
        in_specs=[smem, smem, vmem, vmem] + [pl.BlockSpec(memory_space=pl.ANY)] * count,
        out_specs=[vmem] * (members + 1),
        scratch_shapes=[
            pltpu.VMEM((count * length, width), pieces[0].dtype),
            pltpu.SemaphoreType.DMA((count,)),
        ],
        compiler_params=pltpu.CompilerParams(vmem_limit_bytes=40 * MIB),
        cost_estimate=pl.CostEstimate(
            flops=2 * blocks * members * rows * width * (SPAN + 256),
            bytes_accessed=2
            * (count * length * width + basis.size + blocks * members * rows * width),
            transcendentals=0,
        ),
        name="spectra",
    )(line_index, window_start, basis, total, *pieces)


def power_kernel(total, mix, scale, spectrum, *, blocks, norm_scale):
    padded = total.shape[0] // SUBLANES
    cross = total[...].reshape(padded, SUBLANES, LANES) * norm_scale
    shape = (SUBLANES, LANES)
    lane = lax.broadcasted_iota(jnp.int32, shape, 1)
    sub = lax.broadcasted_iota(jnp.int32, shape, 0)
    place = (lane - sub) & (LANES - 1)
    number = place // 16 + 8 * ((place // 4) % 2)
    is_real = (place // 8) % 2 == 0

    def lane_sum(value):
        for shift in (64, 32, 16, 8, 4):
            value = value + pltpu.roll(value, shift, value.ndim - 1)
        return value

    def turned(vec):
        for_real = jnp.where(is_real, vec, -vec)
        for_imag = jnp.where(is_real, pltpu.roll(vec, LANES - 8, 1), pltpu.roll(vec, 8, 1))
        return for_real, for_imag

    def apply(vec):
        for_real, for_imag = turned(vec)
        out_real = lane_sum(cross * for_real[None])
        out_imag = lane_sum(cross * for_imag[None])
        out = jnp.zeros(shape, jnp.float32)
        for block in range(padded):
            out = jnp.where(number == block, jnp.where(is_real, out_real[block], out_imag[block]), out)
        return out

    vec = jnp.where(is_real & (number < blocks), 1.0 / math.sqrt(blocks), 0.0)
    for _ in range(ITERS):
        out = apply(vec)
        vec = out / jnp.sqrt(lane_sum(out * out))
    value = lane_sum(vec * apply(vec))
    low = vec.astype(jnp.bfloat16).astype(jnp.float32)
    energy = lane_sum(low * apply(low)) * blocks
    factor = lax.rsqrt(jnp.maximum(energy, 0.0) + 1e-06)

    def spread(values, group):
        picked = jnp.where(place % 4 == group, values, 0.0)
        picked = picked + pltpu.roll(picked, 1, 1)
        return picked + pltpu.roll(picked, 2, 1)

    for_real, for_imag = turned(low)
    diagonal = lane % SUBLANES == sub
    for group in range(mix.shape[0]):
        parts = []
        for vec_part in (for_real, for_imag):
            row = []
            for high in range(2):
                shift = (LANES - group - 4 * high) % LANES
                moved = pltpu.roll(vec_part, shift, 1) if shift else vec_part
                row.append(jnp.where(diagonal, moved, 0.0))
            parts.append(jnp.concatenate(row, axis=1))
        mix[group] = jnp.concatenate(parts, axis=0).astype(jnp.bfloat16)
        scale[group] = spread(factor, group)
        spectrum[group] = spread(value, group)


def leading_vectors(total, groups, blocks, norm_scale):
    vmem = pl.BlockSpec(memory_space=pltpu.VMEM)
    return pl.pallas_call(
        functools.partial(power_kernel, blocks=blocks, norm_scale=norm_scale),
        out_shape=[
            jax.ShapeDtypeStruct((groups, GROUP_ROWS, 2 * LANES), jnp.bfloat16),
            jax.ShapeDtypeStruct((groups, SUBLANES, LANES), jnp.float32),
            jax.ShapeDtypeStruct((groups, SUBLANES, LANES), jnp.float32),
        ],
        in_specs=[vmem],
        out_specs=[vmem] * 3,
        name="power",
    )(total)


def modes_kernel(member_ref, mix, scale, *refs, chunks, members):
    coefs = refs[: chunks * members]
    out = refs[chunks * members]
    buffers = refs[chunks * members + 1 : -1]
    sems = refs[-1]
    member = member_ref[0]
    copies = []
    for chunk in range(chunks):
        for turn in range(members):
            slot = lax.rem(member + members - turn, members)
            copy = pltpu.make_async_copy(
                coefs[chunk * members + turn], buffers[chunk].at[slot], sems.at[chunk, turn]
            )
            copy.start()
            copies.append(copy)
    planes = out.shape[2] // members
    done = 0
    for chunk in range(chunks):
        for turn in range(members):
            copies[chunk * members + turn].wait()
        padded, width = buffers[chunk].shape[1], buffers[chunk].shape[3]
        points = width // planes
        for slot in range(members):
            for group in range(mix.shape[0]):
                tile = buffers[chunk][slot, :, group * GROUP_ROWS : (group + 1) * GROUP_ROWS, :]
                tile = tile.reshape(padded * GROUP_ROWS, width)
                raw = jnp.dot(mix[group], tile, preferred_element_type=jnp.float32)
                factor = jnp.tile(scale[group], (1, points // LANES))
                for e in range(2):
                    for plane in range(planes):
                        part = raw[
                            e * SUBLANES : (e + 1) * SUBLANES, plane * points : (plane + 1) * points
                        ]
                        out[
                            e,
                            group * SUBLANES : (group + 1) * SUBLANES,
                            slot * planes + plane,
                            done : done + points,
                        ] = part * factor
        done += points


def project(member, mix, scale, coefs, members, planes):
    chunks = len(coefs) // members
    groups = mix.shape[0]
    points = sum(part.shape[2] for part in coefs[::members]) // planes
    vmem = pl.BlockSpec(memory_space=pltpu.VMEM)
    return pl.pallas_call(
        functools.partial(modes_kernel, chunks=chunks, members=members),
        out_shape=jax.ShapeDtypeStruct(
            (2, groups * SUBLANES, members * planes, points), jnp.float32
        ),
        in_specs=[pl.BlockSpec(memory_space=pltpu.SMEM), vmem, vmem]
        + [pl.BlockSpec(memory_space=pl.ANY)] * len(coefs),
        out_specs=vmem,
        scratch_shapes=[
            pltpu.VMEM((members,) + part.shape, jnp.bfloat16) for part in coefs[::members]
        ]
        + [pltpu.SemaphoreType.DMA((chunks, members))],
        compiler_params=pltpu.CompilerParams(vmem_limit_bytes=48 * MIB),
        name="modes",
    )(member, mix, scale, *coefs)


def chunk_sizes(width):
    if width < 8 * LANES:
        return [LANES] * (width // LANES)
    sizes = [LANES, LANES] + [2 * LANES] * ((width - 4 * LANES) // (2 * LANES)) + [LANES, LANES]
    return sizes


def butterfly_sum(value, axes, count):
    step = 1
    while step < count:
        pairs = [(i, i ^ step) for i in range(count)]
        value = value + lax.ppermute(value, axes, pairs)
        step *= 2
    return value


def shards(series, block_start, freq_index):
    snap_rows, slab_rows, plane = series.shape
    line = ("pts", "sub")
    group_count = lax.axis_size(line)
    members = lax.axis_size("freq")
    member = lax.axis_index("freq")
    width = plane // group_count
    blocks = block_start.shape[0]
    pairs = (blocks + 1) // 2
    frames = snap_rows * group_count
    line_index = lax.axis_index(line).reshape(1)

    order = (member + jnp.arange(members, dtype=jnp.int32)) % members
    freq_order = freq_index.reshape(members, -1)[order].reshape(-1)
    starts = jnp.pad(block_start, (0, 2 * pairs - blocks), mode="edge")
    window_start = jnp.minimum(starts[::2] // 16 * 16, frames - SPAN)
    basis = shifted_basis(freq_order, starts - jnp.repeat(window_start, 2), blocks)

    total = jnp.zeros((members, 2 * pairs * SUBLANES, LANES), jnp.float32)
    sizes = chunk_sizes(width)
    offsets = [sum(sizes[:chunk]) for chunk in range(len(sizes))]
    coefs, pieces, ticket = [], [], line_index

    def exchange(chunk):
        parts = list(prepare(ticket, series, offsets[chunk], sizes[chunk], group_count))
        for piece in range(1, group_count):
            pairs_of_piece = [(i, i ^ piece) for i in range(group_count)]
            parts[piece] = lax.ppermute(parts[piece], line, pairs_of_piece)
        pieces.append(parts)

    for chunk in range(min(AHEAD, len(sizes))):
        exchange(chunk)
    for chunk in range(len(sizes)):
        *sent, total = spectra(line_index, window_start, pieces[chunk], basis, total, members)
        coefs.append(sent[0])
        for turn in range(1, members):
            ring = [(i, (i + turn) % members) for i in range(members)]
            coefs.append(lax.ppermute(sent[turn], "freq", ring))
        if chunk + AHEAD < len(sizes):
            ticket, total = lax.optimization_barrier((ticket, total))
            exchange(chunk + AHEAD)

    mine = total[0]
    for turn in range(1, members):
        ring = [(i, (i + turn) % members) for i in range(members)]
        mine = mine + lax.ppermute(total[turn], "freq", ring)
    mine = butterfly_sum(mine, line, group_count)

    groups = freq_index.shape[0] // members // SUBLANES
    norm_scale = 1.0 / (blocks * slab_rows * members * plane)
    mix, scale, spectrum = leading_vectors(mine, groups, blocks, norm_scale)
    modes = project(member.reshape(1), mix, scale, coefs, members, slab_rows)
    return (modes, spectrum[:, :, 0].reshape(-1))


def solution(mesh):
    in_specs = (P(("pts", "sub"), "freq", "groups"), P(), P())
    out_specs = (P(None, "freq", "groups", ("pts", "sub")), P(("groups", "freq")))
    return jax.shard_map(shards, mesh=mesh, in_specs=in_specs, out_specs=out_specs, check_vma=False)
```

```python
import functools
import math

import jax
import jax.numpy as jnp
from jax import lax
from jax.experimental import pallas as pl
from jax.experimental.pallas import tpu as pltpu
from jax.sharding import PartitionSpec as P

NFFT = 256
ITERS = 3
SPAN = 2 * NFFT
LANES = 128
SUBLANES = 8
SHORT = pl.CostEstimate(flops=1, bytes_accessed=1, transcendentals=0)
PREPARE_ROWS = 64
PREPARE_PIECES = 8
AHEAD = 2
GROUP_ROWS = 2 * SUBLANES
MIB = 1 << 20


def shifted_basis(freq_order, offsets, blocks):
    steps = jnp.arange(SPAN, dtype=jnp.int32)[None, :] - offsets[:, None]
    inside = (steps >= 0) & (steps < NFFT) & (jnp.arange(offsets.shape[0]) < blocks)[:, None]
    steps = jnp.where(inside, steps, 0)
    unit = 2.0 * math.pi / NFFT
    window = 0.5 - 0.5 * jnp.cos(unit * jnp.arange(NFFT, dtype=jnp.int32).astype(jnp.float32))
    shifted_window = 0.5 - 0.5 * jnp.cos(unit * steps.astype(jnp.float32))
    weighting = jnp.where(inside, shifted_window / jnp.sqrt(jnp.sum(window * window)), 0.0)
    freq = freq_order.reshape(1, -1, SUBLANES, 1)
    phase_int = freq * steps[:, None, None, :] % NFFT
    angle = unit * phase_int.astype(jnp.float32)
    table = jnp.stack([jnp.cos(angle), -jnp.sin(angle)], axis=2) * weighting[:, None, None, None, :]
    return table.astype(jnp.bfloat16).reshape(offsets.shape[0] // 2, -1, SPAN)


def prepare_kernel(ticket_ref, *refs, units):
    del ticket_ref
    sources, target = refs[:-1], refs[-1]
    points = units * LANES
    for number, source in enumerate(sources):
        piece, unit = divmod(number, units)
        for plane in range(source.shape[1]):
            first = plane * points + unit * LANES
            target[piece, :, first : first + LANES] = source[:, plane, :]


def prepare(ticket, series, offset, points, count):
    snap_rows, slab_rows, plane = series.shape
    first, stride, units = offset // LANES, plane // count // LANES, points // LANES
    step_rows = min(snap_rows, PREPARE_ROWS)
    together = min(count, PREPARE_PIECES)

    def source_map(piece, unit):
        return lambda part, step, ticket_ref: (
            step,
            0,
            (part * together + piece) * stride + first + unit,
        )

    return pl.pallas_call(
        functools.partial(prepare_kernel, units=units),
        grid_spec=pltpu.PrefetchScalarGridSpec(
            num_scalar_prefetch=1,
            grid=(count // together, snap_rows // step_rows),
            in_specs=[
                pl.BlockSpec((step_rows, slab_rows, LANES), source_map(piece, unit))
                for piece in range(together)
                for unit in range(units)
            ],
            out_specs=pl.BlockSpec(
                (together, step_rows, slab_rows * points),
                lambda part, step, ticket_ref: (part, step, 0),
            ),
        ),
        out_shape=jax.ShapeDtypeStruct((count, snap_rows, slab_rows * points), series.dtype),
        compiler_params=pltpu.CompilerParams(vmem_limit_bytes=40 * MIB),
        cost_estimate=SHORT,
        name="prepare",
    )(ticket, *([series] * (together * units)))


def spectra_kernel(ticket_ref, window_start, history, basis, total_in, *refs, members, unroll):
    del ticket_ref
    coefs = refs[:members]
    total_out = refs[members]
    rows = coefs[0].shape[1]
    pairs = basis.shape[0]
    width = history.shape[1]

    def transform(pair, carry):
        start = pl.multiple_of(window_start[pair], 16)
        segment = history[pl.ds(start, SPAN), :]
        both = jnp.dot(basis[pair], segment, preferred_element_type=jnp.float32)
        both = both.astype(jnp.bfloat16)
        for half in range(2):
            for member in range(members):
                first = (half * members + member) * rows
                coefs[member][2 * pair + half] = both[first : first + rows]
        return carry

    lax.fori_loop(0, pairs, transform, 0, unroll=unroll)
    packed_rows = 2 * pairs * SUBLANES
    lane = lax.broadcasted_iota(jnp.int32, (packed_rows, LANES), 1)
    sub = lax.broadcasted_iota(jnp.int32, (packed_rows, LANES), 0) % SUBLANES
    place = (lane - sub) & (LANES - 1)
    for member in range(members):

        def add_group(group, packed):
            first = pl.multiple_of(group * GROUP_ROWS, GROUP_ROWS)
            tile = coefs[member][:, pl.ds(first, GROUP_ROWS), :]
            tile = tile.reshape(2 * pairs * GROUP_ROWS, width)
            gram = lax.dot_general(
                tile, tile, (((1,), (1,)), ((), ())), preferred_element_type=jnp.float32
            )
            gram = gram.reshape(2 * pairs, 2, SUBLANES, 2 * LANES)
            packed = list(packed)
            for c in range(2):
                for high in range(2):
                    shift = group + 4 * high
                    part = gram[:, c, :, high * LANES : (high + 1) * LANES]
                    part = pltpu.roll(part.reshape(packed_rows, LANES), shift, 1)
                    packed[c] = jnp.where(place % 8 == shift, part, packed[c])
            return tuple(packed)

        empty = jnp.zeros((packed_rows, LANES), jnp.float32)
        packed = lax.fori_loop(0, rows // GROUP_ROWS, add_group, (empty, empty), unroll=unroll)
        swapped = jnp.where(
            (place // 8) % 2 == 0,
            pltpu.roll(packed[1], LANES - 8, 1),
            -pltpu.roll(packed[1], 8, 1),
        )
        total_out[member] = total_in[member] + (packed[0] + swapped)


def spectra(ticket, window_start, history, basis, total, members, unroll):
    width = history.shape[1]
    blocks = 2 * basis.shape[0]
    rows = basis.shape[1] // 2 // members
    smem = pl.BlockSpec(memory_space=pltpu.SMEM)
    vmem = pl.BlockSpec(memory_space=pltpu.VMEM)
    outs = [jax.ShapeDtypeStruct((blocks, rows, width), jnp.bfloat16)] * members
    return pl.pallas_call(
        functools.partial(spectra_kernel, members=members, unroll=unroll),
        out_shape=outs + [jax.ShapeDtypeStruct(total.shape, jnp.float32)],
        in_specs=[smem, smem, vmem, vmem, vmem],
        out_specs=[vmem] * (members + 1),
        compiler_params=pltpu.CompilerParams(vmem_limit_bytes=40 * MIB),
        cost_estimate=SHORT,
        name="spectra",
    )(ticket, window_start, history, basis, total)


def power_kernel(total, mix, scale, spectrum, *, blocks, norm_scale):
    padded = total.shape[0] // SUBLANES
    cross = total[...].reshape(padded, SUBLANES, LANES) * norm_scale
    shape = (SUBLANES, LANES)
    lane = lax.broadcasted_iota(jnp.int32, shape, 1)
    sub = lax.broadcasted_iota(jnp.int32, shape, 0)
    place = (lane - sub) & (LANES - 1)
    number = place // 16 + 8 * ((place // 4) % 2)
    is_real = (place // 8) % 2 == 0

    def lane_sum(value):
        for shift in (64, 32, 16, 8, 4):
            value = value + pltpu.roll(value, shift, value.ndim - 1)
        return value

    def turned(vec):
        for_real = jnp.where(is_real, vec, -vec)
        for_imag = jnp.where(is_real, pltpu.roll(vec, LANES - 8, 1), pltpu.roll(vec, 8, 1))
        return for_real, for_imag

    def apply(vec):
        for_real, for_imag = turned(vec)
        out_real = lane_sum(cross * for_real[None])
        out_imag = lane_sum(cross * for_imag[None])
        out = jnp.zeros(shape, jnp.float32)
        for block in range(padded):
            out = jnp.where(number == block, jnp.where(is_real, out_real[block], out_imag[block]), out)
        return out

    vec = jnp.where(is_real & (number < blocks), 1.0 / math.sqrt(blocks), 0.0)
    for _ in range(ITERS):
        out = apply(vec)
        vec = out / jnp.sqrt(lane_sum(out * out))
    value = lane_sum(vec * apply(vec))
    low = vec.astype(jnp.bfloat16).astype(jnp.float32)
    energy = lane_sum(low * apply(low)) * blocks
    factor = lax.rsqrt(jnp.maximum(energy, 0.0) + 1e-06)

    def spread(values, group):
        picked = jnp.where(place % 4 == group, values, 0.0)
        picked = picked + pltpu.roll(picked, 1, 1)
        return picked + pltpu.roll(picked, 2, 1)

    for_real, for_imag = turned(low)
    diagonal = lane % SUBLANES == sub
    for group in range(mix.shape[0]):
        parts = []
        for vec_part in (for_real, for_imag):
            row = []
            for high in range(2):
                shift = (LANES - group - 4 * high) % LANES
                moved = pltpu.roll(vec_part, shift, 1) if shift else vec_part
                row.append(jnp.where(diagonal, moved, 0.0))
            parts.append(jnp.concatenate(row, axis=1))
        mix[group] = jnp.concatenate(parts, axis=0).astype(jnp.bfloat16)
        scale[group] = spread(factor, group)
        spectrum[group] = spread(value, group)


def leading_vectors(total, groups, blocks, norm_scale):
    vmem = pl.BlockSpec(memory_space=pltpu.VMEM)
    return pl.pallas_call(
        functools.partial(power_kernel, blocks=blocks, norm_scale=norm_scale),
        out_shape=[
            jax.ShapeDtypeStruct((groups, GROUP_ROWS, 2 * LANES), jnp.bfloat16),
            jax.ShapeDtypeStruct((groups, SUBLANES, LANES), jnp.float32),
            jax.ShapeDtypeStruct((groups, SUBLANES, LANES), jnp.float32),
        ],
        in_specs=[vmem],
        out_specs=[vmem] * 3,
        name="power",
    )(total)


def modes_kernel(member_ref, mix, scale, *refs, chunks, members, offset):
    coefs = refs[: chunks * members]
    out = refs[chunks * members + (1 if offset else 0)]
    scratch = refs[-2 * chunks - 2 :]
    buffers, results = scratch[:chunks], scratch[chunks : 2 * chunks]
    sems, out_sems = scratch[2 * chunks :]
    member = member_ref[0]
    copies = []
    for chunk in range(chunks):
        for turn in range(members):
            slot = lax.rem(member + members - turn, members)
            copy = pltpu.make_async_copy(
                coefs[chunk * members + turn], buffers[chunk].at[slot], sems.at[chunk, turn]
            )
            copy.start()
            copies.append(copy)
    planes = out.shape[2] // members
    out_copies = []
    done = offset
    for chunk in range(chunks):
        for turn in range(members):
            copies[chunk * members + turn].wait()
        padded, width = buffers[chunk].shape[1], buffers[chunk].shape[3]
        points = width // planes

        def one_group(group, carry):
            first = pl.multiple_of(group * GROUP_ROWS, GROUP_ROWS)
            factor = jnp.tile(scale[group], (1, points // LANES))
            for slot in range(members):
                tile = buffers[chunk][slot, :, pl.ds(first, GROUP_ROWS), :]
                tile = tile.reshape(padded * GROUP_ROWS, width)
                raw = jnp.dot(mix[group], tile, preferred_element_type=jnp.float32)
                for e in range(2):
                    for plane in range(planes):
                        part = raw[
                            e * SUBLANES : (e + 1) * SUBLANES, plane * points : (plane + 1) * points
                        ]
                        target = pl.ds(pl.multiple_of(group * SUBLANES, SUBLANES), SUBLANES)
                        results[chunk][e, target, slot * planes + plane, :] = part * factor
            return carry

        lax.fori_loop(0, mix.shape[0], one_group, 0)
        copy = pltpu.make_async_copy(
            results[chunk], out.at[:, :, :, pl.ds(done, points)], out_sems.at[chunk]
        )
        copy.start()
        out_copies.append(copy)
        done += points
    for copy in out_copies:
        copy.wait()


def project(member, mix, scale, coefs, members, planes, points, offset, before):
    chunks = len(coefs) // members
    groups = mix.shape[0]
    vmem = pl.BlockSpec(memory_space=pltpu.VMEM)
    hbm = pl.BlockSpec(memory_space=pl.ANY)
    extra = [] if before is None else [before]
    sizes = [part.shape[2] // planes for part in coefs[::members]]
    return pl.pallas_call(
        functools.partial(modes_kernel, chunks=chunks, members=members, offset=offset),
        out_shape=jax.ShapeDtypeStruct(
            (2, groups * SUBLANES, members * planes, points), jnp.float32
        ),
        in_specs=[pl.BlockSpec(memory_space=pltpu.SMEM), vmem, vmem]
        + [hbm] * (len(coefs) + len(extra)),
        out_specs=hbm,
        input_output_aliases={3 + len(coefs): 0} if extra else {},
        scratch_shapes=[
            pltpu.VMEM((members,) + part.shape, jnp.bfloat16) for part in coefs[::members]
        ]
        + [
            pltpu.VMEM((2, groups * SUBLANES, members * planes, size), jnp.float32)
            for size in sizes
        ]
        + [pltpu.SemaphoreType.DMA((chunks, members)), pltpu.SemaphoreType.DMA((chunks,))],
        compiler_params=pltpu.CompilerParams(vmem_limit_bytes=48 * MIB),
        cost_estimate=SHORT,
        name="modes",
    )(member, mix, scale, *coefs, *extra)


def chunk_sizes(width):
    if width % (8 * LANES):
        return [LANES] * (width // LANES)
    quarter = width // (4 * LANES) * LANES
    last = quarter // 2
    return [quarter, width - 2 * quarter - last, quarter, last]


def butterfly_sum(value, axes, count):
    step = 1
    while step < count:
        pairs = [(i, i ^ step) for i in range(count)]
        value = value + lax.ppermute(value, axes, pairs)
        step *= 2
    return value


def shards(series, block_start, freq_index):
    snap_rows, slab_rows, plane = series.shape
    line = ("pts", "sub")
    group_count = lax.axis_size(line)
    members = lax.axis_size("freq")
    member = lax.axis_index("freq")
    width = plane // group_count
    blocks = block_start.shape[0]
    pairs = (blocks + 1) // 2
    frames = snap_rows * group_count

    order = (member + jnp.arange(members, dtype=jnp.int32)) % members
    freq_order = freq_index.reshape(members, -1)[order].reshape(-1)
    starts = jnp.pad(block_start, (0, 2 * pairs - blocks), mode="edge")
    window_start = jnp.minimum(starts[::2] // 16 * 16, frames - SPAN)
    basis = shifted_basis(freq_order, starts - jnp.repeat(window_start, 2), blocks)

    total = jnp.zeros((members, 2 * pairs * SUBLANES, LANES), jnp.float32)
    sizes = chunk_sizes(width)
    offsets = [sum(sizes[:chunk]) for chunk in range(len(sizes))]
    coefs, histories, ticket = [], [], jnp.zeros((1,), jnp.int32)

    prepared = []

    def get_ready(chunk, ticket):
        parts = prepare(ticket, series, offsets[chunk], sizes[chunk], group_count)
        ticket, parts = lax.optimization_barrier((ticket, parts))
        prepared.append(parts)
        return ticket

    def exchange(chunk):
        parts = prepared[chunk]
        if chunk >= 2:
            parts, coefs[chunk - 2][1:] = lax.optimization_barrier((parts, coefs[chunk - 2][1:]))
        history = lax.all_to_all(parts, line, split_axis=0, concat_axis=0, tiled=True)
        histories.append(history.reshape(frames, -1))

    for chunk in range(min(AHEAD, len(sizes))):
        ticket = get_ready(chunk, ticket)
        exchange(chunk)
    for chunk in range(len(sizes)):
        last = chunk + 1 == len(sizes)
        *sent, total = spectra(
            ticket, window_start, histories[chunk], basis, total, members, last
        )
        if chunk + AHEAD < len(sizes):
            ticket, total = lax.optimization_barrier((ticket, total))
            ticket = get_ready(chunk + AHEAD, ticket)
        rings = [[(i, (i + turn) % members) for i in range(members)] for turn in range(members)]
        if last:
            others = [lax.ppermute(total[turn], "freq", rings[turn]) for turn in range(1, members)]
            others, sent[1:] = lax.optimization_barrier((others, sent[1:]))
        for turn in range(1, members):
            sent[turn] = lax.ppermute(sent[turn], "freq", rings[turn])
        coefs.append(sent)
        if chunk + AHEAD < len(sizes):
            exchange(chunk + AHEAD)

    mine = functools.reduce(jnp.add, others, total[0])
    mine = butterfly_sum(mine, line, group_count)

    groups = freq_index.shape[0] // members // SUBLANES
    norm_scale = 1.0 / (blocks * slab_rows * members * plane)
    mix, scale, spectrum = leading_vectors(mine, groups, blocks, norm_scale)
    modes = None
    for chunk_range in (range(len(sizes) - 1), range(len(sizes) - 1, len(sizes))):
        if len(chunk_range):
            parts = [part for chunk in chunk_range for part in coefs[chunk]]
            offset = offsets[chunk_range[0]]
            modes = project(
                member.reshape(1), mix, scale, parts, members, slab_rows, width, offset, modes
            )
    return (modes, spectrum[:, :, 0].reshape(-1))


def solution(mesh):
    in_specs = (P(("pts", "sub"), "freq", "groups"), P(), P())
    out_specs = (P(None, "freq", "groups", ("pts", "sub")), P(("groups", "freq")))
    return jax.shard_map(shards, mesh=mesh, in_specs=in_specs, out_specs=out_specs, check_vma=False)
```

```python
import functools
import math

import jax
import jax.numpy as jnp
from jax import lax
from jax.experimental import pallas as pl
from jax.experimental.pallas import tpu as pltpu
from jax.sharding import PartitionSpec as P

NFFT = 256
ITERS = 3
SPAN = 2 * NFFT
LANES = 128
SUBLANES = 8
SHORT = pl.CostEstimate(flops=1, bytes_accessed=1, transcendentals=0)
PREPARE_ROWS = 64
UNROLL_MODES = 2
PREPARE_PIECES = 8
AHEAD = 2
GROUP_ROWS = 2 * SUBLANES
MIB = 1 << 20


def shifted_basis(freq_order, offsets, blocks):
    steps = jnp.arange(SPAN, dtype=jnp.int32)[None, :] - offsets[:, None]
    inside = (steps >= 0) & (steps < NFFT) & (jnp.arange(offsets.shape[0]) < blocks)[:, None]
    steps = jnp.where(inside, steps, 0)
    unit = 2.0 * math.pi / NFFT
    window = 0.5 - 0.5 * jnp.cos(unit * jnp.arange(NFFT, dtype=jnp.int32).astype(jnp.float32))
    shifted_window = 0.5 - 0.5 * jnp.cos(unit * steps.astype(jnp.float32))
    weighting = jnp.where(inside, shifted_window / jnp.sqrt(jnp.sum(window * window)), 0.0)
    freq = freq_order.reshape(1, -1, SUBLANES, 1)
    phase_int = freq * steps[:, None, None, :] % NFFT
    angle = unit * phase_int.astype(jnp.float32)
    table = jnp.stack([jnp.cos(angle), -jnp.sin(angle)], axis=2) * weighting[:, None, None, None, :]
    return table.astype(jnp.bfloat16).reshape(offsets.shape[0] // 2, -1, SPAN)


def prepare_kernel(ticket_ref, *refs, units):
    del ticket_ref
    sources, target = refs[:-1], refs[-1]
    points = units * LANES
    for number, source in enumerate(sources):
        piece, unit = divmod(number, units)
        by_plane = jnp.transpose(source[...], (1, 0, 2))
        for plane in range(source.shape[1]):
            first = plane * points + unit * LANES
            target[piece, :, first : first + LANES] = by_plane[plane]


def prepare(ticket, series, offset, points, count):
    snap_rows, slab_rows, plane = series.shape
    first, stride, units = offset // LANES, plane // count // LANES, points // LANES
    step_rows = min(snap_rows, PREPARE_ROWS)
    together = min(count, PREPARE_PIECES)

    def source_map(piece, unit):
        return lambda part, step, ticket_ref: (
            step,
            0,
            (part * together + piece) * stride + first + unit,
        )

    return pl.pallas_call(
        functools.partial(prepare_kernel, units=units),
        grid_spec=pltpu.PrefetchScalarGridSpec(
            num_scalar_prefetch=1,
            grid=(count // together, snap_rows // step_rows),
            in_specs=[
                pl.BlockSpec((step_rows, slab_rows, LANES), source_map(piece, unit))
                for piece in range(together)
                for unit in range(units)
            ],
            out_specs=pl.BlockSpec(
                (together, step_rows, slab_rows * points),
                lambda part, step, ticket_ref: (part, step, 0),
            ),
        ),
        out_shape=pltpu.HBM((count, snap_rows, slab_rows * points), series.dtype),
        compiler_params=pltpu.CompilerParams(vmem_limit_bytes=40 * MIB),
        cost_estimate=SHORT,
        name="prepare",
    )(ticket, *([series] * (together * units)))


def spectra_kernel(ticket_ref, window_start, history, basis, total_in, *refs, members, unroll):
    del ticket_ref
    coefs_out = refs[:members]
    total_out, held, *coefs, in_sems, out_sems = refs[members:]
    rows = coefs[0].shape[1]
    pairs = basis.shape[0]
    width = history.shape[1]
    parts = history.shape[0] // NFFT

    def arrival(part):
        rows_of_part = pl.ds(part * NFFT, NFFT)
        return pltpu.make_async_copy(
            history.at[rows_of_part], held.at[rows_of_part], in_sems.at[part]
        )

    def departure(member, pair):
        blocks_of_pair = pl.ds(2 * pair, 2)
        return pltpu.make_async_copy(
            coefs[member].at[blocks_of_pair],
            coefs_out[member].at[blocks_of_pair],
            out_sems.at[member, pair],
        )

    for part in range(parts):
        arrival(part).start()
    for part in range(min(2, parts)):
        arrival(part).wait()

    def transform(pair, carry):
        @pl.when(pair + 2 < parts)
        def _():
            arrival(pair + 2).wait()

        start = pl.multiple_of(window_start[pair], 16)
        segment = held[pl.ds(start, SPAN), :]
        both = jnp.dot(basis[pair], segment, preferred_element_type=jnp.float32)
        both = both.astype(jnp.bfloat16)
        for member in reversed(range(members)):
            for half in range(2):
                first = (half * members + member) * rows
                coefs[member][2 * pair + half] = both[first : first + rows]
            departure(member, pair).start()
        return carry

    lax.fori_loop(0, pairs, transform, 0, unroll=unroll)
    packed_rows = 2 * pairs * SUBLANES
    lane = lax.broadcasted_iota(jnp.int32, (packed_rows, LANES), 1)
    sub = lax.broadcasted_iota(jnp.int32, (packed_rows, LANES), 0) % SUBLANES
    place = (lane - sub) & (LANES - 1)
    for member in range(members):

        def add_group(group, packed):
            first = pl.multiple_of(group * GROUP_ROWS, GROUP_ROWS)
            tile = coefs[member][:, pl.ds(first, GROUP_ROWS), :]
            tile = tile.reshape(2 * pairs * GROUP_ROWS, width)
            gram = lax.dot_general(
                tile, tile, (((1,), (1,)), ((), ())), preferred_element_type=jnp.float32
            )
            gram = gram.reshape(2 * pairs, 2, SUBLANES, 2 * LANES)
            packed = list(packed)
            for c in range(2):
                for high in range(2):
                    shift = group + 4 * high
                    part = gram[:, c, :, high * LANES : (high + 1) * LANES]
                    part = pltpu.roll(part.reshape(packed_rows, LANES), shift, 1)
                    packed[c] = jnp.where(place % 8 == shift, part, packed[c])
            return tuple(packed)

        empty = jnp.zeros((packed_rows, LANES), jnp.float32)
        packed = lax.fori_loop(0, rows // GROUP_ROWS, add_group, (empty, empty), unroll=unroll)
        swapped = jnp.where(
            (place // 8) % 2 == 0,
            pltpu.roll(packed[1], LANES - 8, 1),
            -pltpu.roll(packed[1], 8, 1),
        )
        total_out[member] = total_in[member] + (packed[0] + swapped)
    for member in range(members):
        for pair in range(pairs):
            departure(member, pair).wait()


def spectra(ticket, window_start, history, basis, total, members, unroll):
    frames, width = history.shape
    pairs = basis.shape[0]
    rows = basis.shape[1] // 2 // members
    smem = pl.BlockSpec(memory_space=pltpu.SMEM)
    vmem = pl.BlockSpec(memory_space=pltpu.VMEM)
    hbm = pl.BlockSpec(memory_space=pltpu.HBM)
    shape = (2 * pairs, rows, width)
    return pl.pallas_call(
        functools.partial(spectra_kernel, members=members, unroll=unroll),
        out_shape=[pltpu.HBM(shape, jnp.bfloat16)] * members
        + [jax.ShapeDtypeStruct(total.shape, jnp.float32)],
        in_specs=[smem, smem, hbm, vmem, vmem],
        out_specs=[hbm] * members + [vmem],
        scratch_shapes=[pltpu.VMEM((frames, width), history.dtype)]
        + [pltpu.VMEM(shape, jnp.bfloat16)] * members
        + [
            pltpu.SemaphoreType.DMA((frames // NFFT,)),
            pltpu.SemaphoreType.DMA((members, pairs)),
        ],
        compiler_params=pltpu.CompilerParams(vmem_limit_bytes=40 * MIB),
        cost_estimate=SHORT,
        name="spectra",
    )(ticket, window_start, history, basis, total)


def leading_vectors(total, mix, scale, spectrum, blocks, norm_scale):
    padded = total.shape[0] // SUBLANES
    cross = total[...].reshape(padded, SUBLANES, LANES) * norm_scale
    shape = (SUBLANES, LANES)
    lane = lax.broadcasted_iota(jnp.int32, shape, 1)
    sub = lax.broadcasted_iota(jnp.int32, shape, 0)
    place = (lane - sub) & (LANES - 1)
    number = place // 16 + 8 * ((place // 4) % 2)
    is_real = (place // 8) % 2 == 0

    def lane_sum(value):
        for shift in (64, 32, 16, 8, 4):
            value = value + pltpu.roll(value, shift, value.ndim - 1)
        return value

    def turned(vec):
        for_real = jnp.where(is_real, vec, -vec)
        for_imag = jnp.where(is_real, pltpu.roll(vec, LANES - 8, 1), pltpu.roll(vec, 8, 1))
        return for_real, for_imag

    def apply(vec):
        for_real, for_imag = turned(vec)
        out_real = lane_sum(cross * for_real[None])
        out_imag = lane_sum(cross * for_imag[None])
        out = jnp.zeros(shape, jnp.float32)
        for block in range(padded):
            out = jnp.where(number == block, jnp.where(is_real, out_real[block], out_imag[block]), out)
        return out

    vec = jnp.where(is_real & (number < blocks), 1.0 / math.sqrt(blocks), 0.0)
    for _ in range(ITERS):
        out = apply(vec)
        vec = out / jnp.sqrt(lane_sum(out * out))
    value = lane_sum(vec * apply(vec))
    low = vec.astype(jnp.bfloat16).astype(jnp.float32)
    energy = lane_sum(low * apply(low)) * blocks
    factor = lax.rsqrt(jnp.maximum(energy, 0.0) + 1e-06)

    def spread(values, group):
        picked = jnp.where(place % 4 == group, values, 0.0)
        picked = picked + pltpu.roll(picked, 1, 1)
        return picked + pltpu.roll(picked, 2, 1)

    for_real, for_imag = turned(low)
    diagonal = lane % SUBLANES == sub
    for group in range(mix.shape[0]):
        parts = []
        for vec_part in (for_real, for_imag):
            row = []
            for high in range(2):
                shift = (LANES - group - 4 * high) % LANES
                moved = pltpu.roll(vec_part, shift, 1) if shift else vec_part
                row.append(jnp.where(diagonal, moved, 0.0))
            parts.append(jnp.concatenate(row, axis=1))
        mix[group] = jnp.concatenate(parts, axis=0).astype(jnp.bfloat16)
        scale[group] = spread(factor, group)
        spectrum[group] = spread(value, group)


def modes_kernel(member_ref, *refs, chunks, members, offset, vectors):
    taken = 1 if vectors else 2
    coefs = refs[taken : taken + chunks * members]
    out, *rest = refs[taken + chunks * members + (1 if offset else 0) :]
    if vectors:
        mix, scale, spectrum, *rest = rest
    else:
        mix, scale = refs[:2]
    buffers, results = rest[:chunks], rest[chunks : 2 * chunks]
    sems, out_sems = rest[2 * chunks :]
    member = member_ref[0]
    copies = []
    for chunk in range(chunks):
        for turn in range(members):
            slot = lax.rem(member + members - turn, members)
            copy = pltpu.make_async_copy(
                coefs[chunk * members + turn], buffers[chunk].at[slot], sems.at[chunk, turn]
            )
            copy.start()
            copies.append(copy)
    if vectors:
        leading_vectors(refs[0], mix, scale, spectrum, **vectors)
    planes = out.shape[2] // members
    out_copies = []
    done = offset
    for chunk in range(chunks):
        for turn in range(members):
            copies[chunk * members + turn].wait()
        padded, width = buffers[chunk].shape[1], buffers[chunk].shape[3]
        points = width // planes

        def one_group(group, carry):
            first = pl.multiple_of(group * GROUP_ROWS, GROUP_ROWS)
            factor = jnp.tile(scale[group], (1, points // LANES))
            for slot in range(members):
                tile = buffers[chunk][slot, :, pl.ds(first, GROUP_ROWS), :]
                tile = tile.reshape(padded * GROUP_ROWS, width)
                raw = jnp.dot(mix[group], tile, preferred_element_type=jnp.float32)
                for e in range(2):
                    for plane in range(planes):
                        part = raw[
                            e * SUBLANES : (e + 1) * SUBLANES, plane * points : (plane + 1) * points
                        ]
                        target = pl.ds(pl.multiple_of(group * SUBLANES, SUBLANES), SUBLANES)
                        results[chunk][e, target, slot * planes + plane, :] = part * factor
            return carry

        lax.fori_loop(0, mix.shape[0], one_group, 0, unroll=UNROLL_MODES)
        copy = pltpu.make_async_copy(
            results[chunk], out.at[:, :, :, pl.ds(done, points)], out_sems.at[chunk]
        )
        copy.start()
        out_copies.append(copy)
        done += points
    for copy in out_copies:
        copy.wait()


def project(member, total_or_vectors, coefs, members, planes, shape, offset, before, vectors):
    chunks = len(coefs) // members
    groups = shape[1] // SUBLANES
    vmem = pl.BlockSpec(memory_space=pltpu.VMEM)
    hbm = pl.BlockSpec(memory_space=pltpu.HBM)
    extra = [] if before is None else [before]
    sizes = [part.shape[2] // planes for part in coefs[::members]]
    found = [
        jax.ShapeDtypeStruct((groups, GROUP_ROWS, 2 * LANES), jnp.bfloat16),
        jax.ShapeDtypeStruct((groups, SUBLANES, LANES), jnp.float32),
        jax.ShapeDtypeStruct((groups, SUBLANES, LANES), jnp.float32),
    ]
    found = found if vectors else []
    return pl.pallas_call(
        functools.partial(
            modes_kernel, chunks=chunks, members=members, offset=offset, vectors=vectors
        ),
        out_shape=[pltpu.HBM(shape, jnp.float32)] + found,
        in_specs=[pl.BlockSpec(memory_space=pltpu.SMEM)]
        + [vmem] * len(total_or_vectors)
        + [hbm] * (len(coefs) + len(extra)),
        out_specs=[hbm] + [vmem] * len(found),
        input_output_aliases={1 + len(total_or_vectors) + len(coefs): 0} if extra else {},
        scratch_shapes=[
            pltpu.VMEM((members,) + part.shape, jnp.bfloat16) for part in coefs[::members]
        ]
        + [pltpu.VMEM(shape[:3] + (size,), jnp.float32) for size in sizes]
        + [pltpu.SemaphoreType.DMA((chunks, members)), pltpu.SemaphoreType.DMA((chunks,))],
        compiler_params=pltpu.CompilerParams(vmem_limit_bytes=48 * MIB),
        cost_estimate=SHORT,
        name="modes",
    )(member, *total_or_vectors, *coefs, *extra)


def chunk_sizes(width):
    if width % (8 * LANES):
        return [LANES] * (width // LANES)
    quarter = width // (4 * LANES) * LANES
    last = quarter // 2
    return [quarter, width - 2 * quarter - last, quarter, last]


def butterfly_sum(value, axes, count):
    step = 1
    while step < count:
        pairs = [(i, i ^ step) for i in range(count)]
        value = value + lax.ppermute(value, axes, pairs)
        step *= 2
    return value


def shards(series, block_start, freq_index):
    snap_rows, slab_rows, plane = series.shape
    line = ("pts", "sub")
    group_count = lax.axis_size(line)
    members = lax.axis_size("freq")
    member = lax.axis_index("freq")
    width = plane // group_count
    blocks = block_start.shape[0]
    pairs = (blocks + 1) // 2
    frames = snap_rows * group_count

    order = (member + jnp.arange(members, dtype=jnp.int32)) % members
    freq_order = freq_index.reshape(members, -1)[order].reshape(-1)
    starts = jnp.pad(block_start, (0, 2 * pairs - blocks), mode="edge")
    window_start = jnp.minimum(starts[::2] // 16 * 16, frames - SPAN)
    basis = shifted_basis(freq_order, starts - jnp.repeat(window_start, 2), blocks)

    total = jnp.zeros((members, 2 * pairs * SUBLANES, LANES), jnp.float32)
    sizes = chunk_sizes(width)
    offsets = [sum(sizes[:chunk]) for chunk in range(len(sizes))]
    coefs, histories, ticket = [], [], jnp.zeros((1,), jnp.int32)

    prepared = []

    def get_ready(chunk, ticket):
        parts = prepare(ticket, series, offsets[chunk], sizes[chunk], group_count)
        ticket, parts = lax.optimization_barrier((ticket, parts))
        prepared.append(parts)
        return ticket

    def exchange(chunk):
        parts = prepared[chunk]
        if chunk >= 2:
            parts, coefs[chunk - 2][1:] = lax.optimization_barrier((parts, coefs[chunk - 2][1:]))
        history = lax.all_to_all(parts, line, split_axis=0, concat_axis=0, tiled=True)
        histories.append(history.reshape(frames, -1))

    for chunk in range(min(AHEAD, len(sizes))):
        ticket = get_ready(chunk, ticket)
        exchange(chunk)
    for chunk in range(len(sizes)):
        last = chunk + 1 == len(sizes)
        *sent, total = spectra(
            ticket, window_start, histories[chunk], basis, total, members, True if last else 2
        )
        if chunk + AHEAD < len(sizes):
            ticket, total = lax.optimization_barrier((ticket, total))
            ticket = get_ready(chunk + AHEAD, ticket)
        rings = [[(i, (i + turn) % members) for i in range(members)] for turn in range(members)]
        if last:
            others = [lax.ppermute(total[turn], "freq", rings[turn]) for turn in range(1, members)]
            others, sent[1:] = lax.optimization_barrier((others, sent[1:]))
        for turn in range(1, members):
            sent[turn] = lax.ppermute(sent[turn], "freq", rings[turn])
        coefs.append(sent)
        if chunk + AHEAD < len(sizes):
            exchange(chunk + AHEAD)

    mine = functools.reduce(jnp.add, others, total[0])
    mine = butterfly_sum(mine, line, group_count)

    groups = freq_index.shape[0] // members // SUBLANES
    norm_scale = 1.0 / (blocks * slab_rows * members * plane)
    shape = (2, groups * SUBLANES, members * slab_rows, width)
    early = [part for chunk in coefs[: max(1, len(sizes) - 1)] for part in chunk]
    late = [part for chunk in coefs[max(1, len(sizes) - 1) :] for part in chunk]
    place = member.reshape(1)
    vectors = {"blocks": blocks, "norm_scale": norm_scale}
    modes, mix, scale, spectrum = project(
        place, [mine], early, members, slab_rows, shape, 0, None, vectors
    )
    if late:
        (modes,) = project(
            place, [mix, scale], late, members, slab_rows, shape, offsets[-1], modes, None
        )
    return (modes, spectrum[:, :, 0].reshape(-1))


def solution(mesh):
    in_specs = (P(("pts", "sub"), "freq", "groups"), P(), P())
    out_specs = (P(None, "freq", "groups", ("pts", "sub")), P(("groups", "freq")))
    return jax.shard_map(shards, mesh=mesh, in_specs=in_specs, out_specs=out_specs, check_vma=False)
```

```python
import functools
import math

import jax
import jax.numpy as jnp
from jax import lax
from jax.experimental import pallas as pl
from jax.experimental.pallas import tpu as pltpu
from jax.sharding import PartitionSpec as P

NFFT = 256
ITERS = 3
SPAN = 2 * NFFT
LANES = 128
SUBLANES = 8
SHORT = pl.CostEstimate(flops=1, bytes_accessed=1, transcendentals=0)
PREPARE_ROWS = 64
UNROLL_MODES = 2
PREPARE_PIECES = 8
AHEAD = 2
GROUP_ROWS = 2 * SUBLANES
MIB = 1 << 20


def shifted_basis(freq_order, offsets, blocks):
    steps = jnp.arange(SPAN, dtype=jnp.int32)[None, :] - offsets[:, None]
    inside = (steps >= 0) & (steps < NFFT) & (jnp.arange(offsets.shape[0]) < blocks)[:, None]
    steps = jnp.where(inside, steps, 0)
    unit = 2.0 * math.pi / NFFT
    window = 0.5 - 0.5 * jnp.cos(unit * jnp.arange(NFFT, dtype=jnp.int32).astype(jnp.float32))
    shifted_window = 0.5 - 0.5 * jnp.cos(unit * steps.astype(jnp.float32))
    weighting = jnp.where(inside, shifted_window / jnp.sqrt(jnp.sum(window * window)), 0.0)
    freq = freq_order.reshape(1, -1, SUBLANES, 1)
    phase_int = freq * steps[:, None, None, :] % NFFT
    angle = unit * phase_int.astype(jnp.float32)
    table = jnp.stack([jnp.cos(angle), -jnp.sin(angle)], axis=2) * weighting[:, None, None, None, :]
    return table.astype(jnp.bfloat16).reshape(offsets.shape[0] // 2, -1, SPAN)


def prepare_kernel(ticket_ref, *refs, units):
    del ticket_ref
    sources, target = refs[:-1], refs[-1]
    points = units * LANES
    for number, source in enumerate(sources):
        piece, unit = divmod(number, units)
        by_plane = jnp.transpose(source[...], (1, 0, 2))
        for plane in range(source.shape[1]):
            first = plane * points + unit * LANES
            target[piece, :, first : first + LANES] = by_plane[plane]


def prepare(ticket, series, offset, points, count):
    snap_rows, slab_rows, plane = series.shape
    first, stride, units = offset // LANES, plane // count // LANES, points // LANES
    step_rows = min(snap_rows, PREPARE_ROWS)
    together = min(count, PREPARE_PIECES)

    def source_map(piece, unit):
        return lambda part, step, ticket_ref: (
            step,
            0,
            (part * together + piece) * stride + first + unit,
        )

    return pl.pallas_call(
        functools.partial(prepare_kernel, units=units),
        grid_spec=pltpu.PrefetchScalarGridSpec(
            num_scalar_prefetch=1,
            grid=(count // together, snap_rows // step_rows),
            in_specs=[
                pl.BlockSpec((step_rows, slab_rows, LANES), source_map(piece, unit))
                for piece in range(together)
                for unit in range(units)
            ],
            out_specs=pl.BlockSpec(
                (together, step_rows, slab_rows * points),
                lambda part, step, ticket_ref: (part, step, 0),
            ),
        ),
        out_shape=pltpu.HBM((count, snap_rows, slab_rows * points), series.dtype),
        compiler_params=pltpu.CompilerParams(vmem_limit_bytes=40 * MIB),
        cost_estimate=SHORT,
        name="prepare",
    )(ticket, *([series] * (together * units)))


def spectra_kernel(ticket_ref, window_start, history, basis, total_in, *refs, members, unroll):
    del ticket_ref
    coefs_out = refs[:members]
    total_out, held, *coefs, in_sems, out_sems = refs[members:]
    rows = coefs[0].shape[1]
    pairs = basis.shape[0]
    width = history.shape[1]
    parts = history.shape[0] // NFFT

    def arrival(part):
        rows_of_part = pl.ds(part * NFFT, NFFT)
        return pltpu.make_async_copy(
            history.at[rows_of_part], held.at[rows_of_part], in_sems.at[part]
        )

    def departure(member, pair, count=2):
        blocks_of_pair = pl.ds(2 * pair, count)
        return pltpu.make_async_copy(
            coefs[member].at[blocks_of_pair],
            coefs_out[member].at[blocks_of_pair],
            out_sems.at[member, pair],
        )

    for part in range(parts):
        arrival(part).start()
    for part in range(min(2, parts)):
        arrival(part).wait()

    def transform(pair, carry, kept):
        @pl.when(pair + 2 < parts)
        def _():
            arrival(pair + 2).wait()

        start = pl.multiple_of(window_start[pair], 16)
        segment = held[pl.ds(start, SPAN), :]
        both = jnp.dot(basis[pair], segment, preferred_element_type=jnp.float32)
        both = both.astype(jnp.bfloat16)
        for member in reversed(range(members)):
            for half in range(2):
                first = (half * members + member) * rows
                coefs[member][2 * pair + half] = both[first : first + rows]
            departure(member, pair, kept).start()
        return carry

    last_count = coefs_out[0].shape[0] - 2 * (pairs - 1)
    lax.fori_loop(0, pairs - 1, functools.partial(transform, kept=2), 0, unroll=unroll)
    transform(pairs - 1, 0, last_count)
    packed_rows = 2 * pairs * SUBLANES
    lane = lax.broadcasted_iota(jnp.int32, (packed_rows, LANES), 1)
    sub = lax.broadcasted_iota(jnp.int32, (packed_rows, LANES), 0) % SUBLANES
    place = (lane - sub) & (LANES - 1)
    for member in range(members):

        def add_group(group, packed):
            first = pl.multiple_of(group * GROUP_ROWS, GROUP_ROWS)
            tile = coefs[member][:, pl.ds(first, GROUP_ROWS), :]
            tile = tile.reshape(2 * pairs * GROUP_ROWS, width)
            gram = lax.dot_general(
                tile, tile, (((1,), (1,)), ((), ())), preferred_element_type=jnp.float32
            )
            gram = gram.reshape(2 * pairs, 2, SUBLANES, 2 * LANES)
            packed = list(packed)
            for c in range(2):
                for high in range(2):
                    shift = group + 4 * high
                    part = gram[:, c, :, high * LANES : (high + 1) * LANES]
                    part = pltpu.roll(part.reshape(packed_rows, LANES), shift, 1)
                    packed[c] = jnp.where(place % 8 == shift, part, packed[c])
            return tuple(packed)

        empty = jnp.zeros((packed_rows, LANES), jnp.float32)
        packed = lax.fori_loop(0, rows // GROUP_ROWS, add_group, (empty, empty), unroll=unroll)
        swapped = jnp.where(
            (place // 8) % 2 == 0,
            pltpu.roll(packed[1], LANES - 8, 1),
            -pltpu.roll(packed[1], 8, 1),
        )
        total_out[member] = total_in[member] + (packed[0] + swapped)
    for member in range(members):
        for pair in range(pairs):
            departure(member, pair, 2 if pair + 1 < pairs else last_count).wait()


def spectra(ticket, window_start, history, basis, total, blocks, members, unroll):
    frames, width = history.shape
    pairs = basis.shape[0]
    rows = basis.shape[1] // 2 // members
    smem = pl.BlockSpec(memory_space=pltpu.SMEM)
    vmem = pl.BlockSpec(memory_space=pltpu.VMEM)
    hbm = pl.BlockSpec(memory_space=pltpu.HBM)
    shape = (2 * pairs, rows, width)
    return pl.pallas_call(
        functools.partial(spectra_kernel, members=members, unroll=unroll),
        out_shape=[pltpu.HBM((blocks,) + shape[1:], jnp.bfloat16)] * members
        + [jax.ShapeDtypeStruct(total.shape, jnp.float32)],
        in_specs=[smem, smem, hbm, vmem, vmem],
        out_specs=[hbm] * members + [vmem],
        scratch_shapes=[pltpu.VMEM((frames, width), history.dtype)]
        + [pltpu.VMEM(shape, jnp.bfloat16)] * members
        + [
            pltpu.SemaphoreType.DMA((frames // NFFT,)),
            pltpu.SemaphoreType.DMA((members, pairs)),
        ],
        compiler_params=pltpu.CompilerParams(vmem_limit_bytes=40 * MIB),
        cost_estimate=SHORT,
        name="spectra",
    )(ticket, window_start, history, basis, total)


def leading_vectors(total, mix, scale, spectrum, blocks, norm_scale):
    padded = total.shape[0] // SUBLANES
    cross = total[...].reshape(padded, SUBLANES, LANES) * norm_scale
    shape = (SUBLANES, LANES)
    lane = lax.broadcasted_iota(jnp.int32, shape, 1)
    sub = lax.broadcasted_iota(jnp.int32, shape, 0)
    place = (lane - sub) & (LANES - 1)
    number = place // 16 + 8 * ((place // 4) % 2)
    is_real = (place // 8) % 2 == 0

    def lane_sum(value):
        for shift in (64, 32, 16, 8, 4):
            value = value + pltpu.roll(value, shift, value.ndim - 1)
        return value

    def turned(vec):
        for_real = jnp.where(is_real, vec, -vec)
        for_imag = jnp.where(is_real, pltpu.roll(vec, LANES - 8, 1), pltpu.roll(vec, 8, 1))
        return for_real, for_imag

    def apply(vec):
        for_real, for_imag = turned(vec)
        out_real = lane_sum(cross * for_real[None])
        out_imag = lane_sum(cross * for_imag[None])
        out = jnp.zeros(shape, jnp.float32)
        for block in range(padded):
            out = jnp.where(number == block, jnp.where(is_real, out_real[block], out_imag[block]), out)
        return out

    vec = jnp.where(is_real & (number < blocks), 1.0 / math.sqrt(blocks), 0.0)
    for _ in range(ITERS):
        out = apply(vec)
        vec = out / jnp.sqrt(lane_sum(out * out))
    value = lane_sum(vec * apply(vec))
    low = vec.astype(jnp.bfloat16).astype(jnp.float32)
    energy = lane_sum(low * apply(low)) * blocks
    factor = lax.rsqrt(jnp.maximum(energy, 0.0) + 1e-06)

    def spread(values, group):
        picked = jnp.where(place % 4 == group, values, 0.0)
        picked = picked + pltpu.roll(picked, 1, 1)
        return picked + pltpu.roll(picked, 2, 1)

    for_real, for_imag = turned(low)
    diagonal = lane % SUBLANES == sub
    for group in range(mix.shape[0]):
        parts = []
        for vec_part in (for_real, for_imag):
            row = []
            for high in range(2):
                shift = (LANES - group - 4 * high) % LANES
                moved = pltpu.roll(vec_part, shift, 1) if shift else vec_part
                row.append(jnp.where(diagonal, moved, 0.0))
            parts.append(jnp.concatenate(row, axis=1))
        mix[group] = jnp.concatenate(parts, axis=0).astype(jnp.bfloat16)
        scale[group] = spread(factor, group)
        spectrum[group] = spread(value, group)


def modes_kernel(member_ref, *refs, chunks, members, offset, vectors):
    taken = 1 if vectors else 2
    coefs = refs[taken : taken + chunks * members]
    out, *rest = refs[taken + chunks * members + (1 if offset else 0) :]
    if vectors:
        mix, scale, spectrum, *rest = rest
    else:
        mix, scale = refs[:2]
    buffers, results = rest[:chunks], rest[chunks : 2 * chunks]
    sems, out_sems = rest[2 * chunks :]
    member = member_ref[0]
    copies = []
    for chunk in range(chunks):
        for turn in range(members):
            slot = lax.rem(member + members - turn, members)
            source = coefs[chunk * members + turn]
            copy = pltpu.make_async_copy(
                source, buffers[chunk].at[slot, pl.ds(0, source.shape[0])], sems.at[chunk, turn]
            )
            copy.start()
            copies.append(copy)
    blocks = coefs[0].shape[0]
    for buffer in buffers:
        if blocks < buffer.shape[1]:
            buffer[:, blocks:] = jnp.zeros_like(buffer[:, blocks:])
    if vectors:
        leading_vectors(refs[0], mix, scale, spectrum, **vectors)
    planes = out.shape[2] // members
    out_copies = []
    done = offset
    for chunk in range(chunks):
        for turn in range(members):
            copies[chunk * members + turn].wait()
        padded, width = buffers[chunk].shape[1], buffers[chunk].shape[3]
        points = width // planes

        def one_group(group, carry):
            first = pl.multiple_of(group * GROUP_ROWS, GROUP_ROWS)
            factor = jnp.tile(scale[group], (1, points // LANES))
            for slot in range(members):
                tile = buffers[chunk][slot, :, pl.ds(first, GROUP_ROWS), :]
                tile = tile.reshape(padded * GROUP_ROWS, width)
                raw = jnp.dot(mix[group], tile, preferred_element_type=jnp.float32)
                for e in range(2):
                    for plane in range(planes):
                        part = raw[
                            e * SUBLANES : (e + 1) * SUBLANES, plane * points : (plane + 1) * points
                        ]
                        target = pl.ds(pl.multiple_of(group * SUBLANES, SUBLANES), SUBLANES)
                        results[chunk][e, target, slot * planes + plane, :] = part * factor
            return carry

        lax.fori_loop(0, mix.shape[0], one_group, 0, unroll=UNROLL_MODES)
        copy = pltpu.make_async_copy(
            results[chunk], out.at[:, :, :, pl.ds(done, points)], out_sems.at[chunk]
        )
        copy.start()
        out_copies.append(copy)
        done += points
    for copy in out_copies:
        copy.wait()


def project(member, total_or_vectors, coefs, members, planes, shape, offset, before, vectors):
    chunks = len(coefs) // members
    groups = shape[1] // SUBLANES
    vmem = pl.BlockSpec(memory_space=pltpu.VMEM)
    hbm = pl.BlockSpec(memory_space=pltpu.HBM)
    extra = [] if before is None else [before]
    sizes = [part.shape[2] // planes for part in coefs[::members]]
    found = [
        jax.ShapeDtypeStruct((groups, GROUP_ROWS, 2 * LANES), jnp.bfloat16),
        jax.ShapeDtypeStruct((groups, SUBLANES, LANES), jnp.float32),
        jax.ShapeDtypeStruct((groups, SUBLANES, LANES), jnp.float32),
    ]
    found = found if vectors else []
    return pl.pallas_call(
        functools.partial(
            modes_kernel, chunks=chunks, members=members, offset=offset, vectors=vectors
        ),
        out_shape=[pltpu.HBM(shape, jnp.float32)] + found,
        in_specs=[pl.BlockSpec(memory_space=pltpu.SMEM)]
        + [vmem] * len(total_or_vectors)
        + [hbm] * (len(coefs) + len(extra)),
        out_specs=[hbm] + [vmem] * len(found),
        input_output_aliases={1 + len(total_or_vectors) + len(coefs): 0} if extra else {},
        scratch_shapes=[
            pltpu.VMEM((members, (part.shape[0] + 1) // 2 * 2) + part.shape[1:], jnp.bfloat16)
            for part in coefs[::members]
        ]
        + [pltpu.VMEM(shape[:3] + (size,), jnp.float32) for size in sizes]
        + [pltpu.SemaphoreType.DMA((chunks, members)), pltpu.SemaphoreType.DMA((chunks,))],
        compiler_params=pltpu.CompilerParams(vmem_limit_bytes=48 * MIB),
        cost_estimate=SHORT,
        name="modes",
    )(member, *total_or_vectors, *coefs, *extra)


def chunk_sizes(width):
    if width % (8 * LANES):
        return [LANES] * (width // LANES)
    quarter = width // (4 * LANES) * LANES
    last = quarter // 2
    return [quarter, width - 2 * quarter - last, quarter, last]


def butterfly_sum(value, axes, count):
    def from_distance(distance):
        return lax.ppermute(value, axes, [(i, i ^ distance) for i in range(count)])

    value = value + from_distance(1) if count > 1 else value
    step = 2
    while step < count:
        if 2 * step < count:
            near, far, both = (from_distance(n * step) for n in (1, 2, 3))
            value = (value + near) + (far + both)
        else:
            value = value + from_distance(step)
        step *= 4
    return value


def shards(series, block_start, freq_index):
    snap_rows, slab_rows, plane = series.shape
    line = ("pts", "sub")
    group_count = lax.axis_size(line)
    members = lax.axis_size("freq")
    member = lax.axis_index("freq")
    width = plane // group_count
    blocks = block_start.shape[0]
    pairs = (blocks + 1) // 2
    frames = snap_rows * group_count

    order = (member + jnp.arange(members, dtype=jnp.int32)) % members
    freq_order = freq_index.reshape(members, -1)[order].reshape(-1)
    starts = jnp.pad(block_start, (0, 2 * pairs - blocks), mode="edge")
    window_start = jnp.minimum(starts[::2] // 16 * 16, frames - SPAN)
    basis = shifted_basis(freq_order, starts - jnp.repeat(window_start, 2), blocks)

    total = jnp.zeros((members, 2 * pairs * SUBLANES, LANES), jnp.float32)
    sizes = chunk_sizes(width)
    offsets = [sum(sizes[:chunk]) for chunk in range(len(sizes))]
    coefs, histories, ticket = [], [], jnp.zeros((1,), jnp.int32)

    prepared = []

    def get_ready(chunk, ticket):
        parts = prepare(ticket, series, offsets[chunk], sizes[chunk], group_count)
        ticket, parts = lax.optimization_barrier((ticket, parts))
        prepared.append(parts)
        return ticket

    def exchange(chunk):
        parts = prepared[chunk]
        if chunk >= 2:
            parts, coefs[chunk - 2][1:] = lax.optimization_barrier((parts, coefs[chunk - 2][1:]))
        history = lax.all_to_all(parts, line, split_axis=0, concat_axis=0, tiled=True)
        histories.append(history.reshape(frames, -1))

    for chunk in range(min(AHEAD, len(sizes))):
        ticket = get_ready(chunk, ticket)
        exchange(chunk)
    for chunk in range(len(sizes)):
        last = chunk + 1 == len(sizes)
        *sent, total = spectra(
            ticket,
            window_start,
            histories[chunk],
            basis,
            total,
            blocks,
            members,
            True if last else 2,
        )
        if chunk + AHEAD < len(sizes):
            ticket, total = lax.optimization_barrier((ticket, total))
            ticket = get_ready(chunk + AHEAD, ticket)
        rings = [[(i, (i + turn) % members) for i in range(members)] for turn in range(members)]
        if last:
            others = [lax.ppermute(total[turn], "freq", rings[turn]) for turn in range(1, members)]
            others, sent[1:] = lax.optimization_barrier((others, sent[1:]))
        for turn in range(1, members):
            sent[turn] = lax.ppermute(sent[turn], "freq", rings[turn])
        coefs.append(sent)
        if chunk + AHEAD < len(sizes):
            exchange(chunk + AHEAD)

    mine = functools.reduce(jnp.add, others, total[0])
    mine = butterfly_sum(mine, line, group_count)

    groups = freq_index.shape[0] // members // SUBLANES
    norm_scale = 1.0 / (blocks * slab_rows * members * plane)
    shape = (2, groups * SUBLANES, members * slab_rows, width)
    early = [part for chunk in coefs[: max(1, len(sizes) - 1)] for part in chunk]
    late = [part for chunk in coefs[max(1, len(sizes) - 1) :] for part in chunk]
    place = member.reshape(1)
    vectors = {"blocks": blocks, "norm_scale": norm_scale}
    modes, mix, scale, spectrum = project(
        place, [mine], early, members, slab_rows, shape, 0, None, vectors
    )
    if late:
        (modes,) = project(
            place, [mix, scale], late, members, slab_rows, shape, offsets[-1], modes, None
        )
    return (modes, spectrum[:, :, 0].reshape(-1))


def solution(mesh):
    in_specs = (P(("pts", "sub"), "freq", "groups"), P(), P())
    out_specs = (P(None, "freq", "groups", ("pts", "sub")), P(("groups", "freq")))
    return jax.shard_map(shards, mesh=mesh, in_specs=in_specs, out_specs=out_specs, check_vma=False)
```

```python
import functools
import math

import jax
import jax.numpy as jnp
from jax import lax
from jax.experimental import pallas as pl
from jax.experimental.pallas import tpu as pltpu
from jax.sharding import PartitionSpec as P

NFFT = 256
ITERS = 3
SPAN = 2 * NFFT
LANES = 128
SUBLANES = 8
SHORT = pl.CostEstimate(flops=1, bytes_accessed=1, transcendentals=0)
PREPARE_ROWS = 64
UNROLL_MODES = 4
PREPARE_PIECES = 8
AHEAD = 2
GROUP_ROWS = 2 * SUBLANES
MIB = 1 << 20


def shifted_basis(freq_order, offsets, blocks):
    steps = jnp.arange(SPAN, dtype=jnp.int32)[None, :] - offsets[:, None]
    inside = (steps >= 0) & (steps < NFFT) & (jnp.arange(offsets.shape[0]) < blocks)[:, None]
    steps = jnp.where(inside, steps, 0)
    unit = 2.0 * math.pi / NFFT
    window = 0.5 - 0.5 * jnp.cos(unit * jnp.arange(NFFT, dtype=jnp.int32).astype(jnp.float32))
    shifted_window = 0.5 - 0.5 * jnp.cos(unit * steps.astype(jnp.float32))
    weighting = jnp.where(inside, shifted_window / jnp.sqrt(jnp.sum(window * window)), 0.0)
    freq = freq_order.reshape(1, -1, SUBLANES, 1)
    phase_int = freq * steps[:, None, None, :] % NFFT
    angle = unit * phase_int.astype(jnp.float32)
    table = jnp.stack([jnp.cos(angle), -jnp.sin(angle)], axis=2) * weighting[:, None, None, None, :]
    return table.astype(jnp.bfloat16).reshape(offsets.shape[0] // 2, -1, SPAN)


def prepare_kernel(ticket_ref, *refs, units):
    del ticket_ref
    sources, target = refs[:-1], refs[-1]
    points = units * LANES
    for number, source in enumerate(sources):
        piece, unit = divmod(number, units)
        by_plane = jnp.transpose(source[...], (1, 0, 2))
        for plane in range(source.shape[1]):
            first = plane * points + unit * LANES
            target[piece, :, first : first + LANES] = by_plane[plane]


def prepare(ticket, series, offset, points, count):
    snap_rows, slab_rows, plane = series.shape
    first, stride, units = offset // LANES, plane // count // LANES, points // LANES
    step_rows = min(snap_rows, PREPARE_ROWS)
    together = min(count, PREPARE_PIECES)

    def source_map(piece, unit):
        return lambda part, step, ticket_ref: (
            step,
            0,
            (part * together + piece) * stride + first + unit,
        )

    return pl.pallas_call(
        functools.partial(prepare_kernel, units=units),
        grid_spec=pltpu.PrefetchScalarGridSpec(
            num_scalar_prefetch=1,
            grid=(count // together, snap_rows // step_rows),
            in_specs=[
                pl.BlockSpec((step_rows, slab_rows, LANES), source_map(piece, unit))
                for piece in range(together)
                for unit in range(units)
            ],
            out_specs=pl.BlockSpec(
                (together, step_rows, slab_rows * points),
                lambda part, step, ticket_ref: (part, step, 0),
            ),
        ),
        out_shape=pltpu.HBM((count, snap_rows, slab_rows * points), series.dtype),
        compiler_params=pltpu.CompilerParams(vmem_limit_bytes=40 * MIB),
        cost_estimate=SHORT,
        name="prepare",
    )(ticket, *([series] * (together * units)))


def spectra_kernel(ticket_ref, window_start, history, basis, total_in, *refs, members, unroll):
    del ticket_ref
    coefs_out = refs[:members]
    total_out, held, *coefs, in_sems, out_sems = refs[members:]
    rows = coefs[0].shape[1]
    pairs = basis.shape[0]
    width = history.shape[1]
    parts = history.shape[0] // NFFT

    def arrival(part):
        rows_of_part = pl.ds(part * NFFT, NFFT)
        return pltpu.make_async_copy(
            history.at[rows_of_part], held.at[rows_of_part], in_sems.at[part]
        )

    def departure(member, pair, count=2):
        blocks_of_pair = pl.ds(2 * pair, count)
        return pltpu.make_async_copy(
            coefs[member].at[blocks_of_pair],
            coefs_out[member].at[blocks_of_pair],
            out_sems.at[member, pair],
        )

    for part in range(parts):
        arrival(part).start()
    for part in range(min(2, parts)):
        arrival(part).wait()

    def transform(pair, carry, kept):
        @pl.when(pair + 2 < parts)
        def _():
            arrival(pair + 2).wait()

        start = pl.multiple_of(window_start[pair], 16)
        segment = held[pl.ds(start, SPAN), :]
        both = jnp.dot(basis[pair], segment, preferred_element_type=jnp.float32)
        both = both.astype(jnp.bfloat16)
        for member in reversed(range(members)):
            for half in range(2):
                first = (half * members + member) * rows
                coefs[member][2 * pair + half] = both[first : first + rows]
            departure(member, pair, kept).start()
        return carry

    last_count = coefs_out[0].shape[0] - 2 * (pairs - 1)
    lax.fori_loop(0, pairs - 1, functools.partial(transform, kept=2), 0, unroll=unroll)
    transform(pairs - 1, 0, last_count)
    packed_rows = 2 * pairs * SUBLANES
    lane = lax.broadcasted_iota(jnp.int32, (packed_rows, LANES), 1)
    sub = lax.broadcasted_iota(jnp.int32, (packed_rows, LANES), 0) % SUBLANES
    place = (lane - sub) & (LANES - 1)
    for member in range(members):

        def add_group(group, packed):
            first = pl.multiple_of(group * GROUP_ROWS, GROUP_ROWS)
            tile = coefs[member][:, pl.ds(first, GROUP_ROWS), :]
            tile = tile.reshape(2 * pairs * GROUP_ROWS, width)
            gram = lax.dot_general(
                tile, tile, (((1,), (1,)), ((), ())), preferred_element_type=jnp.float32
            )
            gram = gram.reshape(2 * pairs, 2, SUBLANES, 2 * LANES)
            packed = list(packed)
            for c in range(2):
                for high in range(2):
                    shift = group + 4 * high
                    part = gram[:, c, :, high * LANES : (high + 1) * LANES]
                    part = pltpu.roll(part.reshape(packed_rows, LANES), shift, 1)
                    packed[c] = jnp.where(place % 8 == shift, part, packed[c])
            return tuple(packed)

        empty = jnp.zeros((packed_rows, LANES), jnp.float32)
        packed = lax.fori_loop(0, rows // GROUP_ROWS, add_group, (empty, empty), unroll=unroll)
        swapped = jnp.where(
            (place // 8) % 2 == 0,
            pltpu.roll(packed[1], LANES - 8, 1),
            -pltpu.roll(packed[1], 8, 1),
        )
        total_out[member] = total_in[member] + (packed[0] + swapped)
    for member in range(members):
        for pair in range(pairs):
            departure(member, pair, 2 if pair + 1 < pairs else last_count).wait()


def spectra(ticket, window_start, history, basis, total, blocks, members, unroll):
    frames, width = history.shape
    pairs = basis.shape[0]
    rows = basis.shape[1] // 2 // members
    smem = pl.BlockSpec(memory_space=pltpu.SMEM)
    vmem = pl.BlockSpec(memory_space=pltpu.VMEM)
    hbm = pl.BlockSpec(memory_space=pltpu.HBM)
    shape = (2 * pairs, rows, width)
    return pl.pallas_call(
        functools.partial(spectra_kernel, members=members, unroll=unroll),
        out_shape=[pltpu.HBM((blocks,) + shape[1:], jnp.bfloat16)] * members
        + [jax.ShapeDtypeStruct(total.shape, jnp.float32)],
        in_specs=[smem, smem, hbm, vmem, vmem],
        out_specs=[hbm] * members + [vmem],
        scratch_shapes=[pltpu.VMEM((frames, width), history.dtype)]
        + [pltpu.VMEM(shape, jnp.bfloat16)] * members
        + [
            pltpu.SemaphoreType.DMA((frames // NFFT,)),
            pltpu.SemaphoreType.DMA((members, pairs)),
        ],
        compiler_params=pltpu.CompilerParams(vmem_limit_bytes=40 * MIB),
        cost_estimate=SHORT,
        name="spectra",
    )(ticket, window_start, history, basis, total)


def leading_vectors(total, mix, scale, spectrum, blocks, norm_scale):
    padded = total.shape[0] // SUBLANES
    cross = total[...].reshape(padded, SUBLANES, LANES) * norm_scale
    shape = (SUBLANES, LANES)
    lane = lax.broadcasted_iota(jnp.int32, shape, 1)
    sub = lax.broadcasted_iota(jnp.int32, shape, 0)
    place = (lane - sub) & (LANES - 1)
    number = place // 16 + 8 * ((place // 4) % 2)
    is_real = (place // 8) % 2 == 0

    def lane_sum(value):
        for shift in (64, 32, 16, 8, 4):
            value = value + pltpu.roll(value, shift, value.ndim - 1)
        return value

    def turned(vec):
        for_real = jnp.where(is_real, vec, -vec)
        for_imag = jnp.where(is_real, pltpu.roll(vec, LANES - 8, 1), pltpu.roll(vec, 8, 1))
        return for_real, for_imag

    def apply(vec):
        for_real, for_imag = turned(vec)
        out_real = lane_sum(cross * for_real[None])
        out_imag = lane_sum(cross * for_imag[None])
        out = jnp.zeros(shape, jnp.float32)
        for block in range(padded):
            out = jnp.where(number == block, jnp.where(is_real, out_real[block], out_imag[block]), out)
        return out

    vec = jnp.where(is_real & (number < blocks), 1.0 / math.sqrt(blocks), 0.0)
    for _ in range(ITERS):
        out = apply(vec)
        vec = out / jnp.sqrt(lane_sum(out * out))
    value = lane_sum(vec * apply(vec))
    low = vec.astype(jnp.bfloat16).astype(jnp.float32)
    energy = lane_sum(low * apply(low)) * blocks
    factor = lax.rsqrt(jnp.maximum(energy, 0.0) + 1e-06)

    def spread(values, group):
        picked = jnp.where(place % 4 == group, values, 0.0)
        picked = picked + pltpu.roll(picked, 1, 1)
        return picked + pltpu.roll(picked, 2, 1)

    for_real, for_imag = turned(low)
    diagonal = lane % SUBLANES == sub
    for group in range(mix.shape[0]):
        parts = []
        for vec_part in (for_real, for_imag):
            row = []
            for high in range(2):
                shift = (LANES - group - 4 * high) % LANES
                moved = pltpu.roll(vec_part, shift, 1) if shift else vec_part
                row.append(jnp.where(diagonal, moved, 0.0))
            parts.append(jnp.concatenate(row, axis=1))
        mix[group] = jnp.concatenate(parts, axis=0).astype(jnp.bfloat16)
        scale[group] = spread(factor, group)
        spectrum[group] = spread(value, group)


def modes_kernel(member_ref, *refs, chunks, members, offset, vectors):
    taken = 1 if vectors else 2
    coefs = refs[taken : taken + chunks * members]
    out, *rest = refs[taken + chunks * members + (1 if offset else 0) :]
    if vectors:
        mix, scale, spectrum, *rest = rest
    else:
        mix, scale = refs[:2]
    buffers, results = rest[:chunks], rest[chunks : 2 * chunks]
    sems, out_sems = rest[2 * chunks :]
    member = member_ref[0]
    copies = []
    for chunk in range(chunks):
        for turn in range(members):
            slot = lax.rem(member + members - turn, members)
            source = coefs[chunk * members + turn]
            copy = pltpu.make_async_copy(
                source, buffers[chunk].at[slot, pl.ds(0, source.shape[0])], sems.at[chunk, turn]
            )
            copy.start()
            copies.append(copy)
    blocks = coefs[0].shape[0]
    for buffer in buffers:
        if blocks < buffer.shape[1]:
            buffer[:, blocks:] = jnp.zeros_like(buffer[:, blocks:])
    if vectors:
        leading_vectors(refs[0], mix, scale, spectrum, **vectors)
    planes = out.shape[2] // members
    out_copies = []
    done = offset
    for chunk in range(chunks):
        for turn in range(members):
            copies[chunk * members + turn].wait()
        padded, width = buffers[chunk].shape[1], buffers[chunk].shape[3]
        points = width // planes

        def one_group(group, carry):
            first = pl.multiple_of(group * GROUP_ROWS, GROUP_ROWS)
            factor = jnp.tile(scale[group], (1, points // LANES))
            for slot in range(members):
                tile = buffers[chunk][slot, :, pl.ds(first, GROUP_ROWS), :]
                tile = tile.reshape(padded * GROUP_ROWS, width)
                raw = jnp.dot(mix[group], tile, preferred_element_type=jnp.float32)
                for e in range(2):
                    for plane in range(planes):
                        part = raw[
                            e * SUBLANES : (e + 1) * SUBLANES, plane * points : (plane + 1) * points
                        ]
                        target = pl.ds(pl.multiple_of(group * SUBLANES, SUBLANES), SUBLANES)
                        results[chunk][e, target, slot * planes + plane, :] = part * factor
            return carry

        lax.fori_loop(0, mix.shape[0], one_group, 0, unroll=UNROLL_MODES)
        copy = pltpu.make_async_copy(
            results[chunk], out.at[:, :, :, pl.ds(done, points)], out_sems.at[chunk]
        )
        copy.start()
        out_copies.append(copy)
        done += points
    for copy in out_copies:
        copy.wait()


def project(member, total_or_vectors, coefs, members, planes, shape, offset, before, vectors):
    chunks = len(coefs) // members
    groups = shape[1] // SUBLANES
    vmem = pl.BlockSpec(memory_space=pltpu.VMEM)
    hbm = pl.BlockSpec(memory_space=pltpu.HBM)
    extra = [] if before is None else [before]
    sizes = [part.shape[2] // planes for part in coefs[::members]]
    found = [
        jax.ShapeDtypeStruct((groups, GROUP_ROWS, 2 * LANES), jnp.bfloat16),
        jax.ShapeDtypeStruct((groups, SUBLANES, LANES), jnp.float32),
        jax.ShapeDtypeStruct((groups, SUBLANES, LANES), jnp.float32),
    ]
    found = found if vectors else []
    return pl.pallas_call(
        functools.partial(
            modes_kernel, chunks=chunks, members=members, offset=offset, vectors=vectors
        ),
        out_shape=[pltpu.HBM(shape, jnp.float32)] + found,
        in_specs=[pl.BlockSpec(memory_space=pltpu.SMEM)]
        + [vmem] * len(total_or_vectors)
        + [hbm] * (len(coefs) + len(extra)),
        out_specs=[hbm] + [vmem] * len(found),
        input_output_aliases={1 + len(total_or_vectors) + len(coefs): 0} if extra else {},
        scratch_shapes=[
            pltpu.VMEM((members, (part.shape[0] + 1) // 2 * 2) + part.shape[1:], jnp.bfloat16)
            for part in coefs[::members]
        ]
        + [pltpu.VMEM(shape[:3] + (size,), jnp.float32) for size in sizes]
        + [pltpu.SemaphoreType.DMA((chunks, members)), pltpu.SemaphoreType.DMA((chunks,))],
        compiler_params=pltpu.CompilerParams(vmem_limit_bytes=48 * MIB),
        cost_estimate=SHORT,
        name="modes",
    )(member, *total_or_vectors, *coefs, *extra)


def chunk_sizes(width):
    if width % (8 * LANES):
        return [LANES] * (width // LANES)
    quarter = width // (4 * LANES) * LANES
    last = quarter // 2
    return [quarter, width - 2 * quarter - last, quarter, last]


def butterfly_sum(value, axes, count):
    def from_distance(distance):
        return lax.ppermute(value, axes, [(i, i ^ distance) for i in range(count)])

    value = value + from_distance(1) if count > 1 else value
    step = 2
    while step < count:
        if 2 * step < count:
            near, far, both = (from_distance(n * step) for n in (1, 2, 3))
            value = (value + near) + (far + both)
        else:
            value = value + from_distance(step)
        step *= 4
    return value


def shards(series, block_start, freq_index):
    snap_rows, slab_rows, plane = series.shape
    line = ("pts", "sub")
    group_count = lax.axis_size(line)
    members = lax.axis_size("freq")
    member = lax.axis_index("freq")
    width = plane // group_count
    blocks = block_start.shape[0]
    pairs = (blocks + 1) // 2
    frames = snap_rows * group_count

    order = (member + jnp.arange(members, dtype=jnp.int32)) % members
    freq_order = freq_index.reshape(members, -1)[order].reshape(-1)
    starts = jnp.pad(block_start, (0, 2 * pairs - blocks), mode="edge")
    window_start = jnp.minimum(starts[::2] // 16 * 16, frames - SPAN)
    basis = shifted_basis(freq_order, starts - jnp.repeat(window_start, 2), blocks)

    total = jnp.zeros((members, 2 * pairs * SUBLANES, LANES), jnp.float32)
    sizes = chunk_sizes(width)
    offsets = [sum(sizes[:chunk]) for chunk in range(len(sizes))]
    coefs, histories, ticket = [], [], jnp.zeros((1,), jnp.int32)

    prepared = []

    def get_ready(chunk, ticket):
        parts = prepare(ticket, series, offsets[chunk], sizes[chunk], group_count)
        ticket, parts = lax.optimization_barrier((ticket, parts))
        prepared.append(parts)
        return ticket

    def exchange(chunk):
        parts = prepared[chunk]
        if chunk >= 2:
            parts, coefs[chunk - 2][1:] = lax.optimization_barrier((parts, coefs[chunk - 2][1:]))
        history = lax.all_to_all(parts, line, split_axis=0, concat_axis=0, tiled=True)
        histories.append(history.reshape(frames, -1))

    for chunk in range(min(AHEAD, len(sizes))):
        ticket = get_ready(chunk, ticket)
        exchange(chunk)
    for chunk in range(len(sizes)):
        last = chunk + 1 == len(sizes)
        *sent, total = spectra(
            ticket,
            window_start,
            histories[chunk],
            basis,
            total,
            blocks,
            members,
            True if last else 2,
        )
        if chunk + AHEAD < len(sizes):
            ticket, total = lax.optimization_barrier((ticket, total))
            ticket = get_ready(chunk + AHEAD, ticket)
        rings = [[(i, (i + turn) % members) for i in range(members)] for turn in range(members)]
        if last:
            others = [lax.ppermute(total[turn], "freq", rings[turn]) for turn in range(1, members)]
            others, sent[1:] = lax.optimization_barrier((others, sent[1:]))
        for turn in range(1, members):
            sent[turn] = lax.ppermute(sent[turn], "freq", rings[turn])
        coefs.append(sent)
        if chunk + AHEAD < len(sizes):
            exchange(chunk + AHEAD)

    mine = functools.reduce(jnp.add, others, total[0])
    mine = butterfly_sum(mine, line, group_count)

    groups = freq_index.shape[0] // members // SUBLANES
    norm_scale = 1.0 / (blocks * slab_rows * members * plane)
    shape = (2, groups * SUBLANES, members * slab_rows, width)
    early = [part for chunk in coefs[: max(1, len(sizes) - 1)] for part in chunk]
    late = [part for chunk in coefs[max(1, len(sizes) - 1) :] for part in chunk]
    place = member.reshape(1)
    vectors = {"blocks": blocks, "norm_scale": norm_scale}
    modes, mix, scale, spectrum = project(
        place, [mine], early, members, slab_rows, shape, 0, None, vectors
    )
    if late:
        (modes,) = project(
            place, [mix, scale], late, members, slab_rows, shape, offsets[-1], modes, None
        )
    return (modes, spectrum[:, :, 0].reshape(-1))


def solution(mesh):
    in_specs = (P(("pts", "sub"), "freq", "groups"), P(), P())
    out_specs = (P(None, "freq", "groups", ("pts", "sub")), P(("groups", "freq")))
    return jax.shard_map(shards, mesh=mesh, in_specs=in_specs, out_specs=out_specs, check_vma=False)
```
